512 devices in a mesh: cons: 16 (over y, x), row: 32 (over z, core).
Axes of the slice: x: 4, y: 4, z: 16, core: 2. Of those that a mesh axis runs over, the one named last changes fastest.
Arguments:
- start_primal: float32 [256, 512, 128], P('row', 'cons'), may hold values from 0 to 1
- start_dual: float32 [1024, 128, 128], P(('cons', 'row')), may hold values from 0 to 1
- unit_cost: float32 [256, 512, 128], P('row', 'cons'), may hold values from -6 to 6
- upper_bound: float32 [256, 512, 128], P('row', 'cons'), may hold values from 0.5 to 2
- demand: float32 [1024, 128, 128], P(('cons', 'row')), may hold values from -6 to 6
- tile_values: bfloat16 [8192, 128, 128], P(('cons', 'row')), may hold values from -0.1875 to 0.1875
- tile_rows: int32 [8192], P(('cons', 'row')), may hold values from 0 to 1
- tile_cols: int32 [8192], P(('cons', 'row')), may hold values from 0 to 31
- tile_count: int32 [512], P(('cons', 'row')), may hold values from 8 to 16, as said below
Outputs:
- primal: float32 [256, 512, 128], P('row', 'cons')
- dual: float32 [1024, 128, 128], P(('cons', 'row'))
The draws below stay inside these ranges and needn't reach their ends.
Inputs may be any that keep to these rules, and one draw needn't show every extreme that they name: `tile_count`: A device's live tiles are the first slots of its list; some device has all 16 slots live.
All inputs are finite; a program needn't handle non-finite values.
Results may differ from the reference program's by a relative error of at most 0.00095.
The reference program's roundings to bfloat16 on the way count: a program that leaves them out, or rounds other values in their place, can miss the bound.
Values may be sent and summed in bfloat16 or wider, within the bound.
A program may use at most 128 MiB of HBM per device.

```python
import jax
import jax.numpy as jnp
from jax import lax

SK_DEV = 1
SC = 128
TILE = 128
CB = 2
TMAX = 16
ITERS = 2
NS = 256
NK = 512
VB = 32
NCB = 1024
NT = 8192
N_CONS = 16
N_ROW = 32
DEVICES = 512


def draw_tile_count(key, part):
    counts = jax.random.randint(key, (DEVICES,), TMAX // 2, TMAX + 1)
    fullest = jax.random.randint(jax.random.fold_in(key, 17), (), 0, DEVICES)
    return counts.at[fullest].set(TMAX).astype(jnp.int32)


def plant(entries, rng, low, top_value):
    place = [jax.random.randint(jax.random.fold_in(rng, axis), (), 0, length) for axis, length in enumerate(entries.shape)]
    widest = entries.shape.index(max(entries.shape))
    beside = place[:widest] + [(place[widest] + 1) % entries.shape[widest]] + place[widest + 1:]
    return entries.at[tuple(place)].set(low).at[tuple(beside)].set(top_value)


def block_levels(key, dims, pieces, low, top_value):
    loudness = 1.0
    for dim, parts in pieces:
        steps = jax.random.uniform(jax.random.fold_in(jax.random.fold_in(key, 6), dim), (parts,), jnp.float32, low / len(pieces), top_value / len(pieces))
        loudness = loudness * jnp.repeat(jnp.exp(steps), dims[dim] // parts).reshape((-1,) + (1,) * (len(dims) - 1 - dim))
    return loudness


def bell_draw(key, extent, scale, limit, split=(), kind=jnp.bfloat16):
    drawn = scale * jax.random.normal(key, extent, jnp.float32)
    if split:
        drawn = drawn * block_levels(key, extent, split, -0.22, 0.18)
    return jnp.clip(drawn, -limit, limit).astype(kind)


def setup_inputs(seed: int = 0) -> dict:
    arg_keys = jax.random.split(jax.random.key(seed), 10)
    return {
        "start_primal": jnp.clip(1.0 * jax.random.uniform(arg_keys[0], (NS, NK, SC), jnp.float32) ** block_levels(arg_keys[0], (NS, NK, SC), ((0, 32), (1, 16)), -0.2, 0.2), 0.0, 1.0),
        "start_dual": jnp.clip(1.0 * jax.random.uniform(arg_keys[1], (NCB, TILE, SC), jnp.float32) ** block_levels(arg_keys[1], (NCB, TILE, SC), ((0, 512),), -0.2, 0.2), 0.0, 1.0),
        "unit_cost": bell_draw(arg_keys[2], (NS, NK, SC), 1.0, 6.0, ((0, 32), (1, 16)), jnp.float32),
        "upper_bound": jnp.clip(0.5 + 1.5 * jax.random.uniform(arg_keys[3], (NS, NK, SC), jnp.float32) ** block_levels(arg_keys[3], (NS, NK, SC), ((0, 32), (1, 16)), -0.2, 0.2), 0.5, 2.0),
        "demand": bell_draw(arg_keys[4], (NCB, TILE, SC), 1.0, 6.0, ((0, 512),), jnp.float32),
        "tile_values": bell_draw(arg_keys[5], (NT, TILE, TILE), (TILE * TMAX // CB) ** -0.5, 0.1875, ((0, 512),)),
        "tile_rows": plant(jax.random.randint(arg_keys[6], (NT,), 0, CB), jax.random.fold_in(arg_keys[6], 1), 0, CB - 1).astype(jnp.int32),
        "tile_cols": plant(jax.random.randint(arg_keys[7], (NT,), 0, VB), jax.random.fold_in(arg_keys[7], 1), 0, VB - 1).astype(jnp.int32),
        "tile_count": draw_tile_count(jax.random.fold_in(arg_keys[9], 71), 0),
    }


step_scale = 0.9

def to_panels(values):
    moved = values.reshape(NS, N_CONS, N_ROW, SK_DEV, SC).transpose(2, 1, 3, 0, 4)
    return moved.reshape(N_ROW, VB, TILE, SC)

def from_panels(panels):
    moved = panels.reshape(N_ROW, N_CONS, SK_DEV, NS, SC).transpose(3, 1, 0, 2, 4)
    return moved.reshape(NS, NK, SC)

def forward_all(panels, tiles3, rows2, cols2, tile_count):

    def one_device(device):
        group = device % N_ROW
        blocks = panels[group][cols2[device]].astype(jnp.float32)
        matrix = tiles3[device].astype(jnp.float32)
        product = jnp.einsum('tij,tjs->tis', matrix, blocks, precision=lax.Precision.HIGHEST)
        live = (jnp.arange(TMAX) < tile_count[device]).astype(jnp.float32)
        onehot = (rows2[device][None, :] == jnp.arange(CB)[:, None]).astype(jnp.float32) * live[None, :]
        summed = jnp.dot(onehot, product.reshape(TMAX, TILE * SC), precision=lax.Precision.HIGHEST)
        return summed.reshape(CB, TILE, SC)
    result = lax.map(one_device, jnp.arange(DEVICES))
    return result.reshape(NCB, TILE, SC)

def adjoint_all(dual_low, tiles3, rows2, cols2, tile_count):

    def one_device(total, device):
        group = device % N_ROW
        own = lax.dynamic_slice_in_dim(dual_low, (device * CB).astype(jnp.int32), CB, 0)
        blocks = own[rows2[device]].astype(jnp.float32)
        matrix = tiles3[device].astype(jnp.float32)
        product = jnp.einsum('tij,tis->tjs', matrix, blocks, precision=lax.Precision.HIGHEST)
        live = (jnp.arange(TMAX) < tile_count[device]).astype(jnp.float32)
        onehot = (cols2[device][None, :] == jnp.arange(VB)[:, None]).astype(jnp.float32) * live[None, :]
        summed = jnp.dot(onehot, product.reshape(TMAX, TILE * SC), precision=lax.Precision.HIGHEST)
        total = total.at[group].add(summed.reshape(VB, TILE, SC))
        return (total, None)
    start = jnp.zeros((N_ROW, VB, TILE, SC), jnp.float32)
    total, unused = lax.scan(one_device, start, jnp.arange(DEVICES))
    return from_panels(total)

def reference(start_primal, start_dual, unit_cost, upper_bound, demand, tile_values, tile_rows, tile_cols, tile_count):
    tiles3 = tile_values.reshape(DEVICES, TMAX, TILE, TILE)
    rows2 = tile_rows.reshape(DEVICES, TMAX)
    cols2 = tile_cols.reshape(DEVICES, TMAX)
    primal = start_primal
    dual = start_dual
    weight_ratio = jnp.float32(1.0)
    for iteration in range(ITERS):
        adjoint = adjoint_all(dual.astype(jnp.bfloat16), tiles3, rows2, cols2, tile_count)
        new_primal = jnp.minimum(jnp.maximum(primal - step_scale / weight_ratio * (unit_cost - adjoint), 0.0), upper_bound)
        extrapolated = (2.0 * new_primal - primal).astype(jnp.bfloat16)
        forward = forward_all(to_panels(extrapolated), tiles3, rows2, cols2, tile_count)
        new_dual = jnp.maximum(dual + step_scale * weight_ratio * (demand - forward), 0.0)
        if iteration < ITERS - 1:
            primal_change = jnp.sum((new_primal - primal) ** 2)
            dual_change = jnp.sum((new_dual - dual) ** 2)
            weight_ratio = jnp.sqrt(weight_ratio * jnp.sqrt((dual_change + 1e-06) / (primal_change + 1e-06)))
        primal = new_primal
        dual = new_dual
    return (primal, dual)
```

```python
import functools

import jax
import jax.numpy as jnp
from jax import lax
from jax.experimental import pallas as pl
from jax.experimental.pallas import tpu as pltpu
from jax.sharding import PartitionSpec as P

ITERS = 2
step_scale = 0.9
SIDE = 4
MESH = pl.DeviceIdType.MESH
F32 = jnp.float32
BF16 = jnp.bfloat16
MSGS = 80


def kernel(
    n_row,
    slots,
    meta,
    hot,
    primal_in,
    cost_in,
    bound_in,
    dual_in,
    demand_in,
    tiles,
    primal_out,
    dual_out,
    zs,
    zr,
    chain,
    part,
    r1,
    l1,
    r2,
    l2,
    mid,
    q1r,
    q1l,
    q2r,
    q2l,
    panel,
    newp,
    outb,
    dlow,
    ar_s,
    ar1,
    ar2,
    ar3,
    send_sem,
    recv_sem,
    z_send,
    z_recv,
):
    st_local = primal_in.shape[0] // n_row
    tile = tiles.shape[1]
    half = tile // 2
    me_c = lax.axis_index("cons")
    me_r = lax.axis_index("row")
    y = me_c // SIDE
    x = me_c % SIDE

    def at_xy(yy, xx):
        return lax.rem(yy, SIDE) * SIDE + lax.rem(xx, SIDE)

    x_next, x_prev = at_xy(y, x + 1), at_xy(y, x + 3)
    y_next, y_prev = at_xy(y + 1, x), at_xy(y + 3, x)
    pos_a, pos_b = (x, y), (y, x)
    next_a, prev_a = (x_next, y_next), (x_prev, y_prev)
    next_b, prev_b = (y_next, x_next), (y_prev, x_prev)

    def blk(color, b, a):
        return at_xy(b, a) if color == 0 else at_xy(a, b)

    barrier = pltpu.get_barrier_semaphore()

    def greet(i, carry):
        pl.semaphore_signal(
            barrier, inc=1, device_id=(me_c, lax.rem(me_r + i, n_row)), device_id_type=MESH
        )
        return carry

    for i in range(1, SIDE):
        pl.semaphore_signal(barrier, inc=1, device_id=(at_xy(y, x + i), me_r), device_id_type=MESH)
        pl.semaphore_signal(barrier, inc=1, device_id=(at_xy(y + i, x), me_r), device_id_type=MESH)
    lax.fori_loop(1, n_row, greet, 0)

    pending = []
    counter = [0]

    def send(src, dst, target):
        i = counter[0]
        counter[0] += 1
        copy = pltpu.make_async_remote_copy(
            src_ref=src,
            dst_ref=dst,
            send_sem=send_sem.at[i],
            recv_sem=recv_sem.at[i],
            device_id=(target, me_r),
            device_id_type=MESH,
        )
        copy.start()
        pending.append(copy)
        return copy

    for j in range(n_row):
        for k, ref in enumerate((primal_in, cost_in, bound_in)):
            zs[j, k * st_local : (k + 1) * st_local, :] = ref[pl.ds(j, st_local, stride=n_row), :]

    def adjoint(it):
        for r in range(2):
            src = dual_in if it == 0 else dual_out
            dlow[it, r] = src[r].astype(BF16)
        for t in range(slots):
            row = meta[slots + t]
            prod = lax.dot_general(
                tiles[t], dlow[it, row], (((0,), (0,)), ((), ())), preferred_element_type=F32
            )
            chain[t] = prod + chain[meta[2 * slots + t]]
        for b in range(2 * SIDE * SIDE):
            part[it, b // 2, b % 2] = chain[meta[3 * slots + b]]

    OFF = (2, 1, 3, 0)

    def scatter_sum(it, mids):
        first = {}
        for k in range(4):
            for c in range(2):
                opp = part.at[it, blk(c, pos_b[c] + OFF[k], pos_a[c] + 2), c]
                a = send(opp.at[pl.ds(0, half)], r1.at[it, c, k], next_a[c])
                b = send(opp.at[pl.ds(half, half)], l1.at[it, c, k], prev_a[c])
                first[k, c] = (a, b)
        second = {}
        for k in range(4):
            for c in range(2):
                a, b = first[k, c]
                nb = blk(c, pos_b[c] + OFF[k], pos_a[c] + 1)
                a.wait_recv()
                part[it, nb, c, 0:half, :] = part[it, nb, c, 0:half, :] + r1[it, c, k]
                a2 = send(part.at[it, nb, c], r2.at[it, c, k], next_a[c])
                pb = blk(c, pos_b[c] + OFF[k], pos_a[c] + 3)
                b.wait_recv()
                part[it, pb, c, half:tile, :] = part[it, pb, c, half:tile, :] + l1[it, c, k]
                b2 = send(part.at[it, pb, c], l2.at[it, c, k], prev_a[c])
                second[k, c] = (a2, b2)
        mids(0)
        third, fourth = {}, {}
        for k in range(4):
            for c in range(2):
                a, b = second[k, c]
                a.wait_recv()
                b.wait_recv()
                own = blk(c, pos_b[c] + OFF[k], pos_a[c])
                total = part[it, own, c] + r2[it, c, k] + l2[it, c, k]
                if k == 0:
                    mid[it, c, 0] = total
                    s0 = mid.at[it, c, 0]
                    third[c] = (
                        send(s0.at[pl.ds(0, half)], q1r.at[it, c], next_b[c]),
                        send(s0.at[pl.ds(half, half)], q1l.at[it, c], prev_b[c]),
                    )
                elif k == 1:
                    third[c][0].wait_recv()
                    mid[it, c, 1, half:tile, :] = total[half:tile]
                    mid[it, c, 1, 0:half, :] = total[0:half] + q1r[it, c]
                    fourth[c] = [send(mid.at[it, c, 1], q2r.at[it, c], next_b[c])]
                elif k == 2:
                    third[c][1].wait_recv()
                    mid[it, c, 2, 0:half, :] = total[0:half]
                    mid[it, c, 2, half:tile, :] = total[half:tile] + q1l[it, c]
                    fourth[c].append(send(mid.at[it, c, 2], q2l.at[it, c], prev_b[c]))
                else:
                    mid[it, c, 3] = total
        mids(1)
        return fourth

    def finish_sum(it, c, fourth):
        fourth[c][0].wait_recv()
        fourth[c][1].wait_recv()
        return mid[it, c, 3] + q2r[it, c] + q2l[it, c]

    def gather_start(it, c):
        own = panel.at[it, me_c, c]
        return (
            send(own, own, next_b[c]),
            send(own, own, prev_b[c]),
            send(own, own, next_a[c]),
            send(own, own, prev_a[c]),
        )

    def gather_rest(it, starts):
        lo, hi = pl.ds(0, half), pl.ds(half, half)
        deep = {}
        wide = {c: [(0, starts[c][2], starts[c][3])] for c in range(2)}

        def spread(c, b_off):
            piece = panel.at[it, blk(c, pos_b[c] + b_off, pos_a[c]), c]
            wide[c].append((b_off, send(piece, piece, next_a[c]), send(piece, piece, prev_a[c])))

        for c in range(2):
            starts[c][0].wait_recv()
            piece = panel.at[it, blk(c, pos_b[c] + 3, pos_a[c]), c]
            f = send(piece.at[lo], piece.at[lo], next_b[c])
            starts[c][1].wait_recv()
            piece = panel.at[it, blk(c, pos_b[c] + 1, pos_a[c]), c]
            g = send(piece.at[hi], piece.at[hi], prev_b[c])
            deep[c] = (f, g)
            spread(c, 3)
            spread(c, 1)
        last = []

        def relay(c, entry):
            b_off, f, g = entry
            f.wait_recv()
            piece = panel.at[it, blk(c, pos_b[c] + b_off, pos_a[c] + 3), c]
            last.append(send(piece.at[lo], piece.at[lo], next_a[c]))
            g.wait_recv()
            piece = panel.at[it, blk(c, pos_b[c] + b_off, pos_a[c] + 1), c]
            last.append(send(piece.at[hi], piece.at[hi], prev_a[c]))

        for c in range(2):
            relay(c, wide[c][0])
        for c in range(2):
            deep[c][0].wait_recv()
            deep[c][1].wait_recv()
            spread(c, 2)
        for k in range(1, 4):
            for c in range(2):
                relay(c, wide[c][k])
        for copy in last:
            copy.wait_recv()

    def forward(it, r):
        acc = None
        for t in range(slots):
            prod = jnp.dot(
                tiles[t], panel_at(it, meta[t]), preferred_element_type=F32
            )
            prod = prod * hot[r * slots + t]
            acc = prod if acc is None else acc + prod
        return acc

    def panel_at(it, col):
        return panel[it, col // 2, col % 2]

    chain[slots] = jnp.zeros((tile, tile), F32)
    adjoint(0)
    pl.semaphore_wait(barrier, (n_row - 1) + 2 * (SIDE - 1))

    def row_copy(src, dst, group, i):
        return pltpu.make_async_remote_copy(
            src_ref=src,
            dst_ref=dst,
            send_sem=z_send.at[group],
            recv_sem=z_recv.at[group],
            device_id=(me_c, lax.rem(me_r + i, n_row)),
            device_id_type=MESH,
        )

    def send_in(i, carry):
        row_copy(zs.at[lax.rem(me_r + i, n_row)], zr.at[me_r], 0, i).start()
        return carry

    def wait_rows(buf, group):
        everything = buf.at[pl.ds(0, n_row - 1)]
        pltpu.make_async_copy(everything, everything, z_recv.at[group]).wait()

    def wait_rows_sent(buf, group):
        everything = buf.at[pl.ds(0, n_row - 1)]
        pltpu.make_async_copy(everything, everything, z_send.at[group]).wait()

    lax.fori_loop(1, n_row, send_in, 0)
    zr[me_r] = zs[me_r]
    fourth = scatter_sum(0, lambda stage: None)
    wait_rows(zr, 0)
    starts = {}
    blocks = n_row // 2
    p_change = None
    for c in range(2):
        adj = finish_sum(0, c, fourth)
        rows = pl.ds(c * blocks, blocks)
        old = zr[rows, 0:st_local, :].reshape(tile, tile)
        cost = zr[rows, st_local : 2 * st_local, :].reshape(tile, tile)
        bound = zr[rows, 2 * st_local : 3 * st_local, :].reshape(tile, tile)
        new = jnp.minimum(jnp.maximum(old - step_scale * (cost - adj), 0.0), bound)
        newp[0, c] = new
        panel[0, me_c, c] = (2.0 * new - old).astype(BF16)
        starts[c] = gather_start(0, c)
        moved = jnp.sum((new - old) ** 2, axis=0, keepdims=True)
        p_change = moved if p_change is None else p_change + moved
    gather_rest(0, starts)
    d_change = None
    for r in range(2):
        old = dual_in[r]
        new = jnp.maximum(old + step_scale * (demand_in[r] - forward(0, r)), 0.0)
        dual_out[r] = new
        moved = jnp.sum((new - old) ** 2, axis=0, keepdims=True)
        d_change = moved if d_change is None else d_change + moved
    line = lax.broadcasted_iota(jnp.int32, (8, tile), 0)
    ar_s[0] = jnp.where(
        line == 0,
        jnp.broadcast_to(p_change, (8, tile)),
        jnp.where(line == 1, jnp.broadcast_to(d_change, (8, tile)), 0.0),
    )

    def send_change(i, carry):
        row_copy(ar_s.at[0], ar1.at[me_r], 1, i).start()
        return carry

    lax.fori_loop(1, n_row, send_change, 0)
    ar1[me_r] = ar_s[0]

    adjoint(1)
    counter[0] = MSGS
    sides = {}

    def mids(stage):
        if stage == 0:
            wait_rows(ar1, 1)
            total = ar1[0]
            for i in range(1, n_row):
                total = total + ar1[i]
            ar_s[1] = total
            ar2[x] = total
            sides[0] = [send(ar_s.at[1], ar2.at[x], at_xy(y, x + i)) for i in range(1, SIDE)]
        else:
            for copy in sides[0]:
                copy.wait_recv()
            total = (ar2[0] + ar2[1]) + (ar2[2] + ar2[3])
            ar_s[2] = total
            ar3[y] = total
            sides[1] = [send(ar_s.at[2], ar3.at[y], at_xy(y + i, x)) for i in range(1, SIDE)]

    fourth = scatter_sum(1, mids)
    for copy in sides[1]:
        copy.wait_recv()
    total = (ar3[0] + ar3[1]) + (ar3[2] + ar3[3])
    p_total = jnp.sum(total[0:1], axis=1, keepdims=True)
    d_total = jnp.sum(total[1:2], axis=1, keepdims=True)
    ratio = jnp.sqrt(jnp.sqrt((d_total + 1e-06) / (p_total + 1e-06)))
    p_step = step_scale / ratio
    d_step = step_scale * ratio
    for c in range(2):
        adj = finish_sum(1, c, fourth)
        rows = pl.ds(c * blocks, blocks)
        old = newp[0, c]
        cost = zr[rows, st_local : 2 * st_local, :].reshape(tile, tile)
        bound = zr[rows, 2 * st_local : 3 * st_local, :].reshape(tile, tile)
        new = jnp.minimum(jnp.maximum(old - p_step * (cost - adj), 0.0), bound)
        newp[1, c] = new
        panel[1, me_c, c] = (2.0 * new - old).astype(BF16)
        starts[c] = gather_start(1, c)

    def result_block(j):
        return newp.at[1, j // blocks, pl.ds((j % blocks) * st_local, st_local)]

    def send_out(i, carry):
        row_copy(
            result_block(lax.rem(me_r + i, n_row)),
            outb.at[pl.ds(pl.multiple_of(me_r * st_local, st_local), st_local)],
            2,
            i,
        ).start()
        return carry

    lax.fori_loop(1, n_row, send_out, 0)
    outb[pl.ds(pl.multiple_of(me_r * st_local, st_local), st_local), :] = newp[
        1, me_r // blocks, pl.ds(pl.multiple_of((me_r % blocks) * st_local, st_local), st_local), :
    ]
    gather_rest(1, starts)
    for r in range(2):
        dual_out[r] = jnp.maximum(
            dual_out[r] + d_step * (demand_in[r] - forward(1, r)), 0.0
        )
    everything = outb.at[pl.ds(0, (n_row - 1) * st_local)]
    pltpu.make_async_copy(everything, everything, z_recv.at[2]).wait()
    for s in range(st_local):
        primal_out[s * n_row : (s + 1) * n_row, :] = outb[pl.ds(s, n_row, stride=st_local), :]
    for copy in pending:
        copy.wait_send()
    wait_rows_sent(zs, 0)
    wait_rows_sent(ar1, 1)
    pltpu.make_async_copy(everything, everything, z_send.at[2]).wait()


def body(
    start_primal,
    start_dual,
    unit_cost,
    upper_bound,
    demand,
    tile_values,
    tile_rows,
    tile_cols,
    tile_count,
):
    st_local, sku_local, scenes = start_primal.shape
    n_row = lax.axis_size("row")
    n_cons = lax.axis_size("cons")
    stores = st_local * n_row
    tile = tile_values.shape[1]
    slots = tile_values.shape[0]
    panel_blocks = n_cons * stores // tile
    order = jnp.arange(slots)
    live = order < tile_count[0]
    row_hot = (tile_rows[None, :] == jnp.arange(2)[:, None]) & live[None, :]
    same = (tile_cols[None, :] == tile_cols[:, None]) & (order[None, :] < order[:, None])
    before = jnp.max(jnp.where(same, order[None, :], -1), axis=1)
    before = jnp.where(before < 0, slots, before)
    holds = (tile_cols[None, :] == jnp.arange(panel_blocks)[:, None]) & live[None, :]
    last = jnp.max(jnp.where(holds, order[None, :], -1), axis=1)
    last = jnp.where(last < 0, slots, last)
    meta = jnp.concatenate([tile_cols, tile_rows, before, last]).astype(jnp.int32)
    hot = row_hot.astype(F32).reshape(-1)

    flat = (st_local * sku_local, scenes)
    smem = pl.BlockSpec(memory_space=pltpu.SMEM)
    vmem = pl.BlockSpec(memory_space=pltpu.VMEM)
    total = 2 * MSGS + 2 * (SIDE - 1)
    primal, dual = pl.pallas_call(
        functools.partial(kernel, n_row, slots),
        out_shape=(
            jax.ShapeDtypeStruct(flat, F32),
            jax.ShapeDtypeStruct(start_dual.shape, F32),
        ),
        in_specs=[smem, smem] + [vmem] * 6,
        out_specs=(vmem, vmem),
        scratch_shapes=[
            pltpu.VMEM((n_row, 3 * st_local, scenes), F32),
            pltpu.VMEM((n_row, 3 * st_local, scenes), F32),
            pltpu.VMEM((slots + 1, tile, scenes), F32),
            pltpu.VMEM((2, n_cons, 2, tile, scenes), F32),
            pltpu.VMEM((2, 2, 4, tile // 2, scenes), F32),
            pltpu.VMEM((2, 2, 4, tile // 2, scenes), F32),
            pltpu.VMEM((2, 2, 4, tile, scenes), F32),
            pltpu.VMEM((2, 2, 4, tile, scenes), F32),
            pltpu.VMEM((2, 2, 4, tile, scenes), F32),
            pltpu.VMEM((2, 2, tile // 2, scenes), F32),
            pltpu.VMEM((2, 2, tile // 2, scenes), F32),
            pltpu.VMEM((2, 2, tile, scenes), F32),
            pltpu.VMEM((2, 2, tile, scenes), F32),
            pltpu.VMEM((2, n_cons, 2, tile, scenes), BF16),
            pltpu.VMEM((2, 2, tile, scenes), F32),
            pltpu.VMEM((stores, scenes), F32),
            pltpu.VMEM((2, 2, tile, scenes), BF16),
            pltpu.VMEM((3, 8, scenes), F32),
            pltpu.VMEM((n_row, 8, scenes), F32),
            pltpu.VMEM((SIDE, 8, scenes), F32),
            pltpu.VMEM((SIDE, 8, scenes), F32),
            pltpu.SemaphoreType.DMA((total,)),
            pltpu.SemaphoreType.DMA((total,)),
            pltpu.SemaphoreType.DMA((3,)),
            pltpu.SemaphoreType.DMA((3,)),
        ],
        compiler_params=pltpu.CompilerParams(
            collective_id=0, has_side_effects=True, vmem_limit_bytes=48 * 1024 * 1024
        ),
    )(
        meta,
        hot,
        start_primal.reshape(flat),
        unit_cost.reshape(flat),
        upper_bound.reshape(flat),
        start_dual,
        demand,
        tile_values,
    )
    return (primal.reshape(start_primal.shape), dual)


def solution(mesh):
    placed = (
        P("row", "cons", None),
        P(("cons", "row"), None, None),
        P("row", "cons", None),
        P("row", "cons", None),
        P(("cons", "row"), None, None),
        P(("cons", "row"), None, None),
        P(("cons", "row")),
        P(("cons", "row")),
        P(("cons", "row")),
    )
    return jax.shard_map(
        body,
        mesh=mesh,
        in_specs=placed,
        out_specs=(P("row", "cons", None), P(("cons", "row"), None, None)),
        check_vma=False,
    )
```

```python
import functools

import jax
import jax.numpy as jnp
from jax import lax
from jax.experimental import pallas as pl
from jax.experimental.pallas import tpu as pltpu
from jax.sharding import PartitionSpec as P

ITERS = 2
step_scale = 0.9
SIDE = 4
MESH = pl.DeviceIdType.MESH
F32 = jnp.float32
BF16 = jnp.bfloat16
MSGS = 68


def kernel(
    n_row,
    n_cons,
    slots,
    meta,
    hot,
    primal_hbm,
    cost_hbm,
    bound_hbm,
    dual_hbm,
    demand_hbm,
    tiles_hbm,
    primal_out,
    dual_out,
    zs,
    zr,
    chain,
    part,
    r1,
    l1,
    r2,
    l2,
    mid,
    near,
    panel,
    newp,
    outb,
    dlow,
    ar_s,
    ar1,
    ar2,
    send_sem,
    recv_sem,
    z_send,
    z_recv,
    primal_in,
    cost_in,
    bound_in,
    dual_in,
    demand_in,
    tiles,
    in_sem,
):
    loads = [
        pltpu.make_async_copy(src, dst, in_sem.at[i])
        for i, (src, dst) in enumerate(
            (
                (dual_hbm, dual_in),
                (tiles_hbm, tiles),
                (primal_hbm, primal_in),
                (cost_hbm, cost_in),
                (bound_hbm, bound_in),
                (demand_hbm, demand_in),
            )
        )
    ]
    for load in loads:
        load.start()
    st_local = primal_in.shape[0] // n_row
    tile = tiles.shape[1]
    half = tile // 2
    me_c = lax.axis_index("cons")
    me_r = lax.axis_index("row")
    y = me_c // SIDE
    x = me_c % SIDE

    def at_xy(yy, xx):
        return lax.rem(yy, SIDE) * SIDE + lax.rem(xx, SIDE)

    x_next, x_prev = at_xy(y, x + 1), at_xy(y, x + 3)
    y_next, y_prev = at_xy(y + 1, x), at_xy(y + 3, x)
    pos_a, pos_b = (x, y), (y, x)
    next_a, prev_a = (x_next, y_next), (x_prev, y_prev)

    def blk(color, b, a):
        return at_xy(b, a) if color == 0 else at_xy(a, b)

    def far_first(i):
        step = i // 2
        return n_row // 2 + step - 2 * step * (i % 2)

    barrier = pltpu.get_barrier_semaphore()

    def greet(i, carry):
        pl.semaphore_signal(
            barrier, inc=1, device_id=(me_c, lax.rem(me_r + far_first(i), n_row)), device_id_type=MESH
        )
        return carry

    def greet_cons(i, carry):
        pl.semaphore_signal(
            barrier, inc=1, device_id=(lax.rem(me_c + i, n_cons), me_r), device_id_type=MESH
        )
        return carry

    lax.fori_loop(1, n_row, greet, 0)
    lax.fori_loop(1, n_cons, greet_cons, 0)

    pending = []
    counter = [0]

    def send(src, dst, target):
        i = counter[0]
        counter[0] += 1
        copy = pltpu.make_async_remote_copy(
            src_ref=src,
            dst_ref=dst,
            send_sem=send_sem.at[i],
            recv_sem=recv_sem.at[i],
            device_id=(target, me_r),
            device_id_type=MESH,
        )
        copy.start()
        pending.append(copy)
        return copy

    for load in loads[2:5]:
        load.wait()
    for j in range(n_row):
        for k, ref in enumerate((primal_in, cost_in, bound_in)):
            zs[j, k * st_local : (k + 1) * st_local, :] = ref[pl.ds(j, st_local, stride=n_row), :]

    def adjoint(it):
        for r in range(2):
            src = dual_in if it == 0 else dual_out
            dlow[it, r] = src[r].astype(BF16)
        for t in range(slots):
            row = meta[slots + t]
            prod = lax.dot_general(
                tiles[t], dlow[it, row], (((0,), (0,)), ((), ())), preferred_element_type=F32
            )
            chain[t] = prod + chain[meta[2 * slots + t]]
        for b in range(2 * SIDE * SIDE):
            part[it, b // 2, b % 2] = chain[meta[3 * slots + b]]

    OFF = (2, 1, 3, 0)
    peers_a = [[at_xy(y, x + o), at_xy(y + o, x)] for o in range(SIDE)]
    peers_b = [[at_xy(y + o, x), at_xy(y, x + o)] for o in range(SIDE)]

    def scatter_sum(it, mids):
        first = {}
        for k in range(4):
            for c in range(2):
                opp = part.at[it, blk(c, pos_b[c] + OFF[k], pos_a[c] + 2), c]
                a = send(opp.at[pl.ds(0, half)], r1.at[it, c, k], next_a[c])
                b = send(opp.at[pl.ds(half, half)], l1.at[it, c, k], prev_a[c])
                first[k, c] = (a, b)
        second = {}
        for k in range(4):
            for c in range(2):
                a, b = first[k, c]
                nb = blk(c, pos_b[c] + OFF[k], pos_a[c] + 1)
                a.wait_recv()
                part[it, nb, c, 0:half, :] = part[it, nb, c, 0:half, :] + r1[it, c, k]
                a2 = send(part.at[it, nb, c], r2.at[it, c, k], next_a[c])
                pb = blk(c, pos_b[c] + OFF[k], pos_a[c] + 3)
                b.wait_recv()
                part[it, pb, c, half:tile, :] = part[it, pb, c, half:tile, :] + l1[it, c, k]
                b2 = send(part.at[it, pb, c], l2.at[it, c, k], prev_a[c])
                second[k, c] = (a2, b2)
        mids(0)
        third = {0: [], 1: []}
        for k in range(4):
            for c in range(2):
                a, b = second[k, c]
                a.wait_recv()
                b.wait_recv()
                own = blk(c, pos_b[c] + OFF[k], pos_a[c])
                mid[it, c, k] = part[it, own, c] + r2[it, c, k] + l2[it, c, k]
                if k < 3:
                    third[c].append(
                        send(mid.at[it, c, k], near.at[it, c, k], peers_b[OFF[k]][c])
                    )
        mids(1)
        return third

    def finish_sum(it, c, third):
        for copy in third[c]:
            copy.wait_recv()
        return (mid[it, c, 3] + near[it, c, 0]) + (near[it, c, 1] + near[it, c, 2])

    def gather_start(it, c):
        own = panel.at[it, me_c, c]
        deep = [send(own, own, peers_b[OFF[k]][c]) for k in range(3)]
        wide = [send(own, own, peers_a[OFF[k]][c]) for k in range(3)]
        return deep, wide

    def gather_rest(it, starts):
        wide = []
        for k in (1, 2, 0):
            for c in range(2):
                starts[c][0][k].wait_recv()
                piece = panel.at[it, blk(c, pos_b[c] + SIDE - OFF[k], pos_a[c]), c]
                wide += [send(piece, piece, peers_a[OFF[j]][c]) for j in range(3)]
        for copy in starts[0][1] + starts[1][1] + wide:
            copy.wait_recv()

    def forward(it, r):
        acc = None
        for t in range(slots):
            prod = jnp.dot(
                tiles[t], panel_at(it, meta[t]), preferred_element_type=F32
            )
            prod = prod * hot[r * slots + t]
            acc = prod if acc is None else acc + prod
        return acc

    def panel_at(it, col):
        return panel[it, col // 2, col % 2]

    chain[slots] = jnp.zeros((tile, tile), F32)
    loads[0].wait()
    loads[1].wait()
    adjoint(0)
    loads[5].wait()
    pl.semaphore_wait(barrier, (n_row - 1) + (n_cons - 1))

    def row_copy(src, dst, group, i):
        return pltpu.make_async_remote_copy(
            src_ref=src,
            dst_ref=dst,
            send_sem=z_send.at[group],
            recv_sem=z_recv.at[group],
            device_id=(me_c, lax.rem(me_r + i, n_row)),
            device_id_type=MESH,
        )

    def send_in(n, carry):
        i = far_first(n)
        row_copy(zs.at[lax.rem(me_r + i, n_row)], zr.at[me_r], 0, i).start()
        return carry

    def wait_rows(buf, group):
        everything = buf.at[pl.ds(0, n_row - 1)]
        pltpu.make_async_copy(everything, everything, z_recv.at[group]).wait()

    def wait_rows_sent(buf, group):
        everything = buf.at[pl.ds(0, n_row - 1)]
        pltpu.make_async_copy(everything, everything, z_send.at[group]).wait()

    lax.fori_loop(1, n_row, send_in, 0)
    zr[me_r] = zs[me_r]
    third = scatter_sum(0, lambda stage: None)
    wait_rows(zr, 0)
    starts = {}
    blocks = n_row // 2
    p_change = None
    for c in range(2):
        adj = finish_sum(0, c, third)
        rows = pl.ds(c * blocks, blocks)
        old = zr[rows, 0:st_local, :].reshape(tile, tile)
        cost = zr[rows, st_local : 2 * st_local, :].reshape(tile, tile)
        bound = zr[rows, 2 * st_local : 3 * st_local, :].reshape(tile, tile)
        new = jnp.minimum(jnp.maximum(old - step_scale * (cost - adj), 0.0), bound)
        newp[0, c] = new
        panel[0, me_c, c] = (2.0 * new - old).astype(BF16)
        starts[c] = gather_start(0, c)
        moved = jnp.sum((new - old) ** 2, axis=0, keepdims=True)
        p_change = moved if p_change is None else p_change + moved
    gather_rest(0, starts)
    d_change = None
    for r in range(2):
        old = dual_in[r]
        new = jnp.maximum(old + step_scale * (demand_in[r] - forward(0, r)), 0.0)
        dual_out[r] = new
        moved = jnp.sum((new - old) ** 2, axis=0, keepdims=True)
        d_change = moved if d_change is None else d_change + moved
    lane = lax.broadcasted_iota(jnp.int32, (1, tile), 1)
    p_change = p_change + pltpu.roll(p_change, tile // 2, 1)
    d_change = d_change + pltpu.roll(d_change, tile // 2, 1)
    ar_s[0] = jnp.where(lane < tile // 2, p_change, d_change)

    def send_change(n, carry):
        i = far_first(n)
        row_copy(ar_s.at[0], ar1.at[me_r], 1, i).start()
        return carry

    lax.fori_loop(1, n_row, send_change, 0)
    ar1[me_r] = ar_s[0]

    adjoint(1)
    counter[0] = MSGS

    def cons_copy(i):
        return pltpu.make_async_remote_copy(
            src_ref=ar_s.at[1],
            dst_ref=ar2.at[me_c],
            send_sem=z_send.at[3],
            recv_sem=z_recv.at[3],
            device_id=(lax.rem(me_c + i, n_cons), me_r),
            device_id_type=MESH,
        )

    def send_cons(i, carry):
        cons_copy(i).start()
        return carry

    def mids(stage):
        if stage == 0:
            wait_rows(ar1, 1)
            total = jnp.sum(ar1[...], axis=0)
            ar_s[1] = total
            ar2[me_c] = total
            lax.fori_loop(1, n_cons, send_cons, 0)

    third = scatter_sum(1, mids)
    others = ar2.at[pl.ds(0, n_cons - 1)]
    pltpu.make_async_copy(others, others, z_recv.at[3]).wait()
    total = jnp.sum(ar2[...], axis=0)
    p_total = jnp.sum(jnp.where(lane < tile // 2, total, 0.0), axis=1, keepdims=True)
    d_total = jnp.sum(jnp.where(lane < tile // 2, 0.0, total), axis=1, keepdims=True)
    ratio = jnp.sqrt(jnp.sqrt((d_total + 1e-06) / (p_total + 1e-06)))
    p_step = step_scale / ratio
    d_step = step_scale * ratio
    for c in range(2):
        adj = finish_sum(1, c, third)
        rows = pl.ds(c * blocks, blocks)
        old = newp[0, c]
        cost = zr[rows, st_local : 2 * st_local, :].reshape(tile, tile)
        bound = zr[rows, 2 * st_local : 3 * st_local, :].reshape(tile, tile)
        new = jnp.minimum(jnp.maximum(old - p_step * (cost - adj), 0.0), bound)
        newp[1, c] = new
        panel[1, me_c, c] = (2.0 * new - old).astype(BF16)
        starts[c] = gather_start(1, c)

    def result_block(j):
        return newp.at[1, j // blocks, pl.ds((j % blocks) * st_local, st_local)]

    def send_out(n, carry):
        i = far_first(n)
        row_copy(
            result_block(lax.rem(me_r + i, n_row)),
            outb.at[pl.ds(pl.multiple_of(me_r * st_local, st_local), st_local)],
            2,
            i,
        ).start()
        return carry

    lax.fori_loop(1, n_row, send_out, 0)
    outb[pl.ds(pl.multiple_of(me_r * st_local, st_local), st_local), :] = newp[
        1, me_r // blocks, pl.ds(pl.multiple_of((me_r % blocks) * st_local, st_local), st_local), :
    ]
    gather_rest(1, starts)
    for r in range(2):
        dual_out[r] = jnp.maximum(
            dual_out[r] + d_step * (demand_in[r] - forward(1, r)), 0.0
        )
    everything = outb.at[pl.ds(0, (n_row - 1) * st_local)]
    pltpu.make_async_copy(everything, everything, z_recv.at[2]).wait()
    for s in range(st_local):
        primal_out[s * n_row : (s + 1) * n_row, :] = outb[pl.ds(s, n_row, stride=st_local), :]
    for copy in pending:
        copy.wait_send()
    wait_rows_sent(zs, 0)
    wait_rows_sent(ar1, 1)
    pltpu.make_async_copy(others, others, z_send.at[3]).wait()
    pltpu.make_async_copy(everything, everything, z_send.at[2]).wait()


def body(
    start_primal,
    start_dual,
    unit_cost,
    upper_bound,
    demand,
    tile_values,
    tile_rows,
    tile_cols,
    tile_count,
):
    st_local, sku_local, scenes = start_primal.shape
    n_row = lax.axis_size("row")
    n_cons = lax.axis_size("cons")
    stores = st_local * n_row
    tile = tile_values.shape[1]
    slots = tile_values.shape[0]
    panel_blocks = n_cons * stores // tile
    order = jnp.arange(slots)
    live = order < tile_count[0]
    row_hot = (tile_rows[None, :] == jnp.arange(2)[:, None]) & live[None, :]
    same = (tile_cols[None, :] == tile_cols[:, None]) & (order[None, :] < order[:, None])
    before = jnp.max(jnp.where(same, order[None, :], -1), axis=1)
    before = jnp.where(before < 0, slots, before)
    holds = (tile_cols[None, :] == jnp.arange(panel_blocks)[:, None]) & live[None, :]
    last = jnp.max(jnp.where(holds, order[None, :], -1), axis=1)
    last = jnp.where(last < 0, slots, last)
    meta = jnp.concatenate([tile_cols, tile_rows, before, last]).astype(jnp.int32)
    hot = row_hot.astype(F32).reshape(-1)

    flat = (st_local * sku_local, scenes)
    smem = pl.BlockSpec(memory_space=pltpu.SMEM)
    vmem = pl.BlockSpec(memory_space=pltpu.VMEM)
    primal, dual = pl.pallas_call(
        functools.partial(kernel, n_row, n_cons, slots),
        out_shape=(
            jax.ShapeDtypeStruct(flat, F32),
            jax.ShapeDtypeStruct(start_dual.shape, F32),
        ),
        in_specs=[smem, smem] + [pl.BlockSpec(memory_space=pltpu.MemorySpace.HBM)] * 6,
        out_specs=(vmem, vmem),
        scratch_shapes=[
            pltpu.VMEM((n_row, 3 * st_local, scenes), F32),
            pltpu.VMEM((n_row, 3 * st_local, scenes), F32),
            pltpu.VMEM((slots + 1, tile, scenes), F32),
            pltpu.VMEM((2, n_cons, 2, tile, scenes), F32),
            pltpu.VMEM((2, 2, 4, tile // 2, scenes), F32),
            pltpu.VMEM((2, 2, 4, tile // 2, scenes), F32),
            pltpu.VMEM((2, 2, 4, tile, scenes), F32),
            pltpu.VMEM((2, 2, 4, tile, scenes), F32),
            pltpu.VMEM((2, 2, 4, tile, scenes), F32),
            pltpu.VMEM((2, 2, 3, tile, scenes), F32),
            pltpu.VMEM((2, n_cons, 2, tile, scenes), BF16),
            pltpu.VMEM((2, 2, tile, scenes), F32),
            pltpu.VMEM((stores, scenes), F32),
            pltpu.VMEM((2, 2, tile, scenes), BF16),
            pltpu.VMEM((2, 1, scenes), F32),
            pltpu.VMEM((n_row, 1, scenes), F32),
            pltpu.VMEM((n_cons, 1, scenes), F32),
            pltpu.SemaphoreType.DMA((2 * MSGS,)),
            pltpu.SemaphoreType.DMA((2 * MSGS,)),
            pltpu.SemaphoreType.DMA((4,)),
            pltpu.SemaphoreType.DMA((4,)),
            pltpu.VMEM(flat, F32),
            pltpu.VMEM(flat, F32),
            pltpu.VMEM(flat, F32),
            pltpu.VMEM(start_dual.shape, F32),
            pltpu.VMEM(demand.shape, F32),
            pltpu.VMEM(tile_values.shape, BF16),
            pltpu.SemaphoreType.DMA((6,)),
        ],
        compiler_params=pltpu.CompilerParams(
            collective_id=0, has_side_effects=True, vmem_limit_bytes=48 * 1024 * 1024
        ),
    )(
        meta,
        hot,
        start_primal.reshape(flat),
        unit_cost.reshape(flat),
        upper_bound.reshape(flat),
        start_dual,
        demand,
        tile_values,
    )
    return (primal.reshape(start_primal.shape), dual)


def solution(mesh):
    placed = (
        P("row", "cons", None),
        P(("cons", "row"), None, None),
        P("row", "cons", None),
        P("row", "cons", None),
        P(("cons", "row"), None, None),
        P(("cons", "row"), None, None),
        P(("cons", "row")),
        P(("cons", "row")),
        P(("cons", "row")),
    )
    return jax.shard_map(
        body,
        mesh=mesh,
        in_specs=placed,
        out_specs=(P("row", "cons", None), P(("cons", "row"), None, None)),
        check_vma=False,
    )
```

```python
import functools

import jax
import jax.numpy as jnp
from jax import lax
from jax.experimental import pallas as pl
from jax.experimental.pallas import tpu as pltpu
from jax.sharding import PartitionSpec as P

ITERS = 2
step_scale = 0.9
SIDE = 4
MESH = pl.DeviceIdType.MESH
F32 = jnp.float32
BF16 = jnp.bfloat16
MSGS = 84


def kernel(
    n_row,
    n_cons,
    slots,
    rows_ref,
    cols_ref,
    count_ref,
    primal_hbm,
    cost_hbm,
    bound_hbm,
    dual_hbm,
    demand_hbm,
    tiles_hbm,
    primal_out,
    dual_out,
    zs,
    zr,
    chain,
    part,
    r1,
    l1,
    r2,
    l2,
    mid,
    near,
    panel,
    newp,
    outb,
    dlow,
    ar_s,
    ar1,
    ar2,
    send_sem,
    recv_sem,
    z_send,
    z_recv,
    primal_in,
    cost_in,
    bound_in,
    dual_in,
    demand_in,
    tiles,
    in_sem,
):
    loads = [
        pltpu.make_async_copy(src, dst, in_sem.at[i])
        for i, (src, dst) in enumerate(
            (
                (dual_hbm, dual_in),
                (tiles_hbm, tiles),
                (primal_hbm, primal_in),
                (cost_hbm, cost_in),
                (bound_hbm, bound_in),
                (demand_hbm, demand_in),
            )
        )
    ]
    for load in loads:
        load.start()
    st_local = primal_in.shape[0] // n_row
    tile = tiles.shape[1]
    half = tile // 2
    me_c = lax.axis_index("cons")
    me_r = lax.axis_index("row")
    y = me_c // SIDE
    x = me_c % SIDE

    def at_xy(yy, xx):
        return lax.rem(yy, SIDE) * SIDE + lax.rem(xx, SIDE)

    x_next, x_prev = at_xy(y, x + 1), at_xy(y, x + 3)
    y_next, y_prev = at_xy(y + 1, x), at_xy(y + 3, x)
    pos_a, pos_b = (x, y), (y, x)
    next_a, prev_a = (x_next, y_next), (x_prev, y_prev)

    def blk(color, b, a):
        return at_xy(b, a) if color == 0 else at_xy(a, b)

    def far_first(i):
        step = i // 2
        return n_row // 2 + step - 2 * step * (i % 2)

    barrier = pltpu.get_barrier_semaphore()

    def greet(n, carry):
        peer = lax.rem(me_r + far_first(n), n_row)
        pl.semaphore_signal(barrier, inc=1, device_id=(me_c, peer), device_id_type=MESH)
        return carry

    lax.fori_loop(1, n_row, greet, 0)
    for peer in (x_next, x_prev, y_next, y_prev):
        pl.semaphore_signal(barrier, inc=1, device_id=(peer, me_r), device_id_type=MESH)

    pending = []
    counter = [0]

    def send(src, dst, target):
        i = counter[0]
        counter[0] += 1
        copy = pltpu.make_async_remote_copy(
            src_ref=src,
            dst_ref=dst,
            send_sem=send_sem.at[i],
            recv_sem=recv_sem.at[i],
            device_id=(target, me_r),
            device_id_type=MESH,
        )
        copy.start()
        pending.append(copy)
        return copy

    count = count_ref[0]
    rows = [rows_ref[t] for t in range(slots)]
    cols = [cols_ref[t] for t in range(slots)]
    live = [jnp.where(t < count, cols[t], -1) for t in range(slots)]
    before = []
    for t in range(slots):
        found = jnp.int32(slots)
        for u in range(t):
            found = jnp.where(cols[u] == cols[t], u, found)
        before.append(found)
    last_tile = []
    for b in range(2 * n_cons):
        found = jnp.int32(slots)
        for t in range(slots):
            found = jnp.where(live[t] == b, t, found)
        last_tile.append(found)
    hot = [
        [jnp.where((rows[t] == r) & (t < count), 1.0, 0.0).astype(F32) for t in range(slots)]
        for r in range(2)
    ]

    for load in loads[2:5]:
        load.wait()
    for j in range(n_row):
        for k, ref in enumerate((primal_in, cost_in, bound_in)):
            zs[j, k * st_local : (k + 1) * st_local, :] = ref[pl.ds(j, st_local, stride=n_row), :]

    def adjoint(it):
        for r in range(2):
            src = dual_in if it == 0 else dual_out
            dlow[it, r] = src[r].astype(BF16)
        for t in range(slots):
            prod = lax.dot_general(
                tiles[t], dlow[it, rows[t]], (((0,), (0,)), ((), ())), preferred_element_type=F32
            )
            chain[t] = prod + chain[before[t]]
        for b in range(2 * n_cons):
            part[it, b // 2, b % 2] = chain[last_tile[b]]

    OFF = (2, 1, 3, 0)
    peers_a = [[at_xy(y, x + o), at_xy(y + o, x)] for o in range(SIDE)]
    peers_b = [[at_xy(y + o, x), at_xy(y, x + o)] for o in range(SIDE)]

    def scatter_sum(it, between):
        lo, hi = pl.ds(0, half), pl.ds(half, half)
        first, early, second = {}, {}, {}
        third = {0: [], 1: []}

        def chunk(k, c, step):
            return blk(c, pos_b[c] + OFF[k], pos_a[c] + step)

        def ahead(k):
            for c in range(2):
                up = part.at[it, chunk(k, c, 1), c]
                down = part.at[it, chunk(k, c, 3), c]
                early[k, c] = (
                    send(up.at[hi], r2.at[it, c, k].at[hi], next_a[c]),
                    send(down.at[lo], l2.at[it, c, k].at[lo], prev_a[c]),
                )

        for k in range(4):
            for c in range(2):
                opp = part.at[it, chunk(k, c, 2), c]
                first[k, c] = (
                    send(opp.at[lo], r1.at[it, c, k], next_a[c]),
                    send(opp.at[hi], l1.at[it, c, k], prev_a[c]),
                )
        ahead(0)
        ahead(1)
        between(0)
        for k in range(4):
            for c in range(2):
                up, down = chunk(k, c, 1), chunk(k, c, 3)
                first[k, c][0].wait_recv()
                part[it, up, c, 0:half, :] = part[it, up, c, 0:half, :] + r1[it, c, k]
                a = send(part.at[it, up, c].at[lo], r2.at[it, c, k].at[lo], next_a[c])
                first[k, c][1].wait_recv()
                part[it, down, c, half:tile, :] = part[it, down, c, half:tile, :] + l1[it, c, k]
                b = send(part.at[it, down, c].at[hi], l2.at[it, c, k].at[hi], prev_a[c])
                second[k, c] = (a, b)
            if k < 2:
                ahead(k + 2)
            between(1 + k)
        for k in range(4):
            for c in range(2):
                for copy in early[k, c] + second[k, c]:
                    copy.wait_recv()
                own = chunk(k, c, 0)
                mid[it, c, k] = part[it, own, c] + r2[it, c, k] + l2[it, c, k]
                if k < 3:
                    third[c].append(
                        send(mid.at[it, c, k], near.at[it, c, k], peers_b[OFF[k]][c])
                    )
            between(5 + k)
        return third

    def finish_sum(it, c, third):
        for copy in third[c]:
            copy.wait_recv()
        return (mid[it, c, 3] + near[it, c, 0]) + (near[it, c, 1] + near[it, c, 2])

    def gather_start(it, c):
        own = panel.at[it, me_c, c]
        deep = [send(own, own, peers_b[OFF[k]][c]) for k in range(3)]
        wide = [send(own, own, peers_a[OFF[k]][c]) for k in range(3)]
        return deep, wide

    def gather_rest(it, starts):
        wide = []
        for k in (1, 2, 0):
            for c in range(2):
                starts[c][0][k].wait_recv()
                piece = panel.at[it, blk(c, pos_b[c] + SIDE - OFF[k], pos_a[c]), c]
                wide += [send(piece, piece, peers_a[OFF[j]][c]) for j in range(3)]
        for copy in starts[0][1] + starts[1][1] + wide:
            copy.wait_recv()

    def forward(it, r):
        acc = None
        for t in range(slots):
            prod = jnp.dot(
                tiles[t], panel_at(it, cols[t]), preferred_element_type=F32
            )
            prod = prod * hot[r][t]
            acc = prod if acc is None else acc + prod
        return acc

    def panel_at(it, col):
        return panel[it, col // 2, col % 2]

    chain[slots] = jnp.zeros((tile, tile), F32)
    loads[0].wait()
    loads[1].wait()
    adjoint(0)
    loads[5].wait()
    pl.semaphore_wait(barrier, n_row - 1 + 4)

    def row_copy(src, dst, group, i):
        return pltpu.make_async_remote_copy(
            src_ref=src,
            dst_ref=dst,
            send_sem=z_send.at[group],
            recv_sem=z_recv.at[group],
            device_id=(me_c, lax.rem(me_r + i, n_row)),
            device_id_type=MESH,
        )

    def send_in(n, carry):
        i = far_first(n)
        row_copy(zs.at[lax.rem(me_r + i, n_row)], zr.at[me_r], 0, i).start()
        return carry

    def wait_rows(buf, group):
        everything = buf.at[pl.ds(0, n_row - 1)]
        pltpu.make_async_copy(everything, everything, z_recv.at[group]).wait()

    def wait_rows_sent(buf, group):
        everything = buf.at[pl.ds(0, n_row - 1)]
        pltpu.make_async_copy(everything, everything, z_send.at[group]).wait()

    lax.fori_loop(1, n_row, send_in, 0)
    zr[me_r] = zs[me_r]
    third = scatter_sum(0, lambda stage: None)
    wait_rows(zr, 0)
    starts = {}
    blocks = n_row // 2
    p_change = None
    for c in range(2):
        adj = finish_sum(0, c, third)
        span = pl.ds(c * blocks, blocks)
        old = zr[span, 0:st_local, :].reshape(tile, tile)
        cost = zr[span, st_local : 2 * st_local, :].reshape(tile, tile)
        bound = zr[span, 2 * st_local : 3 * st_local, :].reshape(tile, tile)
        new = jnp.minimum(jnp.maximum(old - step_scale * (cost - adj), 0.0), bound)
        newp[0, c] = new
        panel[0, me_c, c] = (2.0 * new - old).astype(BF16)
        starts[c] = gather_start(0, c)
        moved = jnp.sum((new - old) ** 2, axis=0, keepdims=True)
        p_change = moved if p_change is None else p_change + moved
    gather_rest(0, starts)
    d_change = None
    for r in range(2):
        old = dual_in[r]
        new = jnp.maximum(old + step_scale * (demand_in[r] - forward(0, r)), 0.0)
        dual_out[r] = new
        moved = jnp.sum((new - old) ** 2, axis=0, keepdims=True)
        d_change = moved if d_change is None else d_change + moved
    lane = lax.broadcasted_iota(jnp.int32, (1, tile), 1)
    p_change = p_change + pltpu.roll(p_change, tile // 2, 1)
    d_change = d_change + pltpu.roll(d_change, tile // 2, 1)
    ar_s[0] = jnp.where(lane < tile // 2, p_change, d_change)

    def send_change(n, carry):
        i = far_first(n)
        row_copy(ar_s.at[0], ar1.at[me_r], 1, i).start()
        return carry

    lax.fori_loop(1, n_row, send_change, 0)
    ar1[me_r] = ar_s[0]

    adjoint(1)
    counter[0] = MSGS

    def cons_copy(i):
        return pltpu.make_async_remote_copy(
            src_ref=ar_s.at[1],
            dst_ref=ar2.at[me_c],
            send_sem=z_send.at[3],
            recv_sem=z_recv.at[3],
            device_id=(lax.rem(me_c + i, n_cons), me_r),
            device_id_type=MESH,
        )

    def send_cons(i, carry):
        cons_copy(i).start()
        return carry

    def between_second(stage):
        if stage == 6:
            wait_rows(ar1, 1)
            total = jnp.sum(ar1[...], axis=0)
            ar_s[1] = total
            ar2[me_c] = total
            lax.fori_loop(1, n_cons, send_cons, 0)

    third = scatter_sum(1, between_second)
    others = ar2.at[pl.ds(0, n_cons - 1)]
    pltpu.make_async_copy(others, others, z_recv.at[3]).wait()
    total = jnp.sum(ar2[...], axis=0)
    p_total = jnp.sum(jnp.where(lane < tile // 2, total, 0.0), axis=1, keepdims=True)
    d_total = jnp.sum(jnp.where(lane < tile // 2, 0.0, total), axis=1, keepdims=True)
    ratio = jnp.sqrt(jnp.sqrt((d_total + 1e-06) / (p_total + 1e-06)))
    p_step = step_scale / ratio
    d_step = step_scale * ratio
    for c in range(2):
        adj = finish_sum(1, c, third)
        span = pl.ds(c * blocks, blocks)
        old = newp[0, c]
        cost = zr[span, st_local : 2 * st_local, :].reshape(tile, tile)
        bound = zr[span, 2 * st_local : 3 * st_local, :].reshape(tile, tile)
        new = jnp.minimum(jnp.maximum(old - p_step * (cost - adj), 0.0), bound)
        newp[1, c] = new
        panel[1, me_c, c] = (2.0 * new - old).astype(BF16)
        starts[c] = gather_start(1, c)

    def result_block(j):
        return newp.at[1, j // blocks, pl.ds((j % blocks) * st_local, st_local)]

    def send_out(n, carry):
        i = far_first(n)
        row_copy(
            result_block(lax.rem(me_r + i, n_row)),
            outb.at[pl.ds(pl.multiple_of(me_r * st_local, st_local), st_local)],
            2,
            i,
        ).start()
        return carry

    lax.fori_loop(1, n_row, send_out, 0)
    outb[pl.ds(pl.multiple_of(me_r * st_local, st_local), st_local), :] = newp[
        1, me_r // blocks, pl.ds(pl.multiple_of((me_r % blocks) * st_local, st_local), st_local), :
    ]
    gather_rest(1, starts)
    for r in range(2):
        dual_out[r] = jnp.maximum(
            dual_out[r] + d_step * (demand_in[r] - forward(1, r)), 0.0
        )
    everything = outb.at[pl.ds(0, (n_row - 1) * st_local)]
    pltpu.make_async_copy(everything, everything, z_recv.at[2]).wait()
    for s in range(st_local):
        primal_out[s * n_row : (s + 1) * n_row, :] = outb[pl.ds(s, n_row, stride=st_local), :]
    for copy in pending:
        copy.wait_send()
    wait_rows_sent(zs, 0)
    wait_rows_sent(ar1, 1)
    pltpu.make_async_copy(others, others, z_send.at[3]).wait()
    pltpu.make_async_copy(everything, everything, z_send.at[2]).wait()


def body(
    start_primal,
    start_dual,
    unit_cost,
    upper_bound,
    demand,
    tile_values,
    tile_rows,
    tile_cols,
    tile_count,
):
    st_local, sku_local, scenes = start_primal.shape
    n_row = lax.axis_size("row")
    n_cons = lax.axis_size("cons")
    stores = st_local * n_row
    tile = tile_values.shape[1]
    slots = tile_values.shape[0]
    flat = (st_local * sku_local, scenes)
    smem = pl.BlockSpec(memory_space=pltpu.SMEM)
    vmem = pl.BlockSpec(memory_space=pltpu.VMEM)
    primal, dual = pl.pallas_call(
        functools.partial(kernel, n_row, n_cons, slots),
        out_shape=(
            jax.ShapeDtypeStruct(flat, F32),
            jax.ShapeDtypeStruct(start_dual.shape, F32),
        ),
        in_specs=[smem, smem, smem] + [pl.BlockSpec(memory_space=pltpu.MemorySpace.HBM)] * 6,
        out_specs=(vmem, vmem),
        scratch_shapes=[
            pltpu.VMEM((n_row, 3 * st_local, scenes), F32),
            pltpu.VMEM((n_row, 3 * st_local, scenes), F32),
            pltpu.VMEM((slots + 1, tile, scenes), F32),
            pltpu.VMEM((2, n_cons, 2, tile, scenes), F32),
            pltpu.VMEM((2, 2, 4, tile // 2, scenes), F32),
            pltpu.VMEM((2, 2, 4, tile // 2, scenes), F32),
            pltpu.VMEM((2, 2, 4, tile, scenes), F32),
            pltpu.VMEM((2, 2, 4, tile, scenes), F32),
            pltpu.VMEM((2, 2, 4, tile, scenes), F32),
            pltpu.VMEM((2, 2, 3, tile, scenes), F32),
            pltpu.VMEM((2, n_cons, 2, tile, scenes), BF16),
            pltpu.VMEM((2, 2, tile, scenes), F32),
            pltpu.VMEM((stores, scenes), F32),
            pltpu.VMEM((2, 2, tile, scenes), BF16),
            pltpu.VMEM((2, 1, scenes), F32),
            pltpu.VMEM((n_row, 1, scenes), F32),
            pltpu.VMEM((n_cons, 1, scenes), F32),
            pltpu.SemaphoreType.DMA((2 * MSGS,)),
            pltpu.SemaphoreType.DMA((2 * MSGS,)),
            pltpu.SemaphoreType.DMA((4,)),
            pltpu.SemaphoreType.DMA((4,)),
            pltpu.VMEM(flat, F32),
            pltpu.VMEM(flat, F32),
            pltpu.VMEM(flat, F32),
            pltpu.VMEM(start_dual.shape, F32),
            pltpu.VMEM(demand.shape, F32),
            pltpu.VMEM(tile_values.shape, BF16),
            pltpu.SemaphoreType.DMA((6,)),
        ],
        compiler_params=pltpu.CompilerParams(
            collective_id=0, has_side_effects=True, vmem_limit_bytes=67_043_328
        ),
    )(
        tile_rows,
        tile_cols,
        tile_count,
        start_primal.reshape(flat),
        unit_cost.reshape(flat),
        upper_bound.reshape(flat),
        start_dual,
        demand,
        tile_values,
    )
    return (primal.reshape(start_primal.shape), dual)


def solution(mesh):
    placed = (
        P("row", "cons", None),
        P(("cons", "row"), None, None),
        P("row", "cons", None),
        P("row", "cons", None),
        P(("cons", "row"), None, None),
        P(("cons", "row"), None, None),
        P(("cons", "row")),
        P(("cons", "row")),
        P(("cons", "row")),
    )
    return jax.shard_map(
        body,
        mesh=mesh,
        in_specs=placed,
        out_specs=(P("row", "cons", None), P(("cons", "row"), None, None)),
        check_vma=False,
    )
```

```python
import functools

import jax
import jax.numpy as jnp
from jax import lax
from jax.experimental import pallas as pl
from jax.experimental.pallas import tpu as pltpu
from jax.sharding import PartitionSpec as P

ITERS = 2
step_scale = 0.9
SIDE = 4
MESH = pl.DeviceIdType.MESH
F32 = jnp.float32
BF16 = jnp.bfloat16
MSGS = 84


PRIMAL = (0.0, 1.0, 20)
COST = (-6.0, 6.0, 22)
BOUND = (0.5, 2.0, 20)
SPLIT = 9


def fixed(value, form):
    low, high, bits = form
    top = float((1 << bits) - 1)
    code = (value - low) * (top / (high - low)) + 0.5
    return jnp.clip(code, 0.0, top).astype(jnp.int32)


def unfixed(code, form):
    low, high, bits = form
    return code.astype(F32) * ((high - low) / float((1 << bits) - 1)) + low


def kernel(
    n_row,
    n_cons,
    slots,
    rows_ref,
    cols_ref,
    count_ref,
    primal_hbm,
    cost_hbm,
    bound_hbm,
    dual_hbm,
    demand_hbm,
    tiles_hbm,
    primal_out,
    dual_out,
    zs,
    zr,
    chain,
    part,
    r1,
    l1,
    r2,
    l2,
    mid,
    near,
    panel,
    newp,
    outb,
    dlow,
    ar_s,
    ar1,
    ar2,
    send_sem,
    recv_sem,
    z_send,
    z_recv,
    primal_in,
    cost_in,
    bound_in,
    dual_in,
    demand_in,
    tiles,
    in_sem,
):
    loads = [
        pltpu.make_async_copy(src, dst, in_sem.at[i])
        for i, (src, dst) in enumerate(
            (
                (dual_hbm, dual_in),
                (tiles_hbm, tiles),
                (primal_hbm, primal_in),
                (cost_hbm, cost_in),
                (bound_hbm, bound_in),
                (demand_hbm, demand_in),
            )
        )
    ]
    for load in loads:
        load.start()
    st_local = primal_in.shape[0] // n_row
    tile = tiles.shape[1]
    half = tile // 2
    me_c = lax.axis_index("cons")
    me_r = lax.axis_index("row")
    y = me_c // SIDE
    x = me_c % SIDE

    def at_xy(yy, xx):
        return lax.rem(yy, SIDE) * SIDE + lax.rem(xx, SIDE)

    x_next, x_prev = at_xy(y, x + 1), at_xy(y, x + 3)
    y_next, y_prev = at_xy(y + 1, x), at_xy(y + 3, x)
    pos_a, pos_b = (x, y), (y, x)
    next_a, prev_a = (x_next, y_next), (x_prev, y_prev)

    def blk(color, b, a):
        return at_xy(b, a) if color == 0 else at_xy(a, b)

    def far_first(i):
        step = i // 2
        return n_row // 2 + step - 2 * step * (i % 2)

    barrier = pltpu.get_barrier_semaphore()

    def greet(n, carry):
        peer = lax.rem(me_r + far_first(n), n_row)
        pl.semaphore_signal(barrier, inc=1, device_id=(me_c, peer), device_id_type=MESH)
        return carry

    lax.fori_loop(1, n_row, greet, 0)
    for peer in (x_next, x_prev, y_next, y_prev):
        pl.semaphore_signal(barrier, inc=1, device_id=(peer, me_r), device_id_type=MESH)

    pending = []
    counter = [0]

    def send(src, dst, target):
        i = counter[0]
        counter[0] += 1
        copy = pltpu.make_async_remote_copy(
            src_ref=src,
            dst_ref=dst,
            send_sem=send_sem.at[i],
            recv_sem=recv_sem.at[i],
            device_id=(target, me_r),
            device_id_type=MESH,
        )
        copy.start()
        pending.append(copy)
        return copy

    count = count_ref[0]
    rows = [rows_ref[t] for t in range(slots)]
    cols = [cols_ref[t] for t in range(slots)]
    live = [jnp.where(t < count, cols[t], -1) for t in range(slots)]
    before = []
    for t in range(slots):
        found = jnp.int32(slots)
        for u in range(t):
            found = jnp.where(cols[u] == cols[t], u, found)
        before.append(found)
    last_tile = []
    for b in range(2 * n_cons):
        found = jnp.int32(slots)
        for t in range(slots):
            found = jnp.where(live[t] == b, t, found)
        last_tile.append(found)
    hot = [
        [jnp.where((rows[t] == r) & (t < count), 1.0, 0.0).astype(F32) for t in range(slots)]
        for r in range(2)
    ]

    for load in loads[2:5]:
        load.wait()
    for j in range(n_row):
        stores = pl.ds(j, st_local, stride=n_row)
        start = fixed(primal_in[stores, :], PRIMAL)
        cost = fixed(cost_in[stores, :], COST)
        bound = fixed(bound_in[stores, :], BOUND)
        zs[j, 0:st_local, :] = cost * (1 << SPLIT) + (bound >> (BOUND[2] - SPLIT))
        rest = bound & ((1 << (BOUND[2] - SPLIT)) - 1)
        zs[j, st_local : 2 * st_local, :] = rest * (1 << PRIMAL[2]) + start

    def adjoint(it):
        for r in range(2):
            src = dual_in if it == 0 else dual_out
            dlow[it, r] = src[r].astype(BF16)
        for t in range(slots):
            prod = lax.dot_general(
                tiles[t], dlow[it, rows[t]], (((0,), (0,)), ((), ())), preferred_element_type=F32
            )
            chain[t] = prod + chain[before[t]]
        for b in range(2 * n_cons):
            part[it, b // 2, b % 2] = chain[last_tile[b]]

    OFF = (2, 1, 3, 0)
    peers_a = [[at_xy(y, x + o), at_xy(y + o, x)] for o in range(SIDE)]
    peers_b = [[at_xy(y + o, x), at_xy(y, x + o)] for o in range(SIDE)]

    def scatter_sum(it, between):
        lo, hi = pl.ds(0, half), pl.ds(half, half)
        first, early, second = {}, {}, {}
        third = {0: [], 1: []}

        def chunk(k, c, step):
            return blk(c, pos_b[c] + OFF[k], pos_a[c] + step)

        def ahead(k):
            for c in range(2):
                up = part.at[it, chunk(k, c, 1), c]
                down = part.at[it, chunk(k, c, 3), c]
                early[k, c] = (
                    send(up.at[hi], r2.at[it, c, k].at[hi], next_a[c]),
                    send(down.at[lo], l2.at[it, c, k].at[lo], prev_a[c]),
                )

        for k in range(4):
            for c in range(2):
                opp = part.at[it, chunk(k, c, 2), c]
                first[k, c] = (
                    send(opp.at[lo], r1.at[it, c, k], next_a[c]),
                    send(opp.at[hi], l1.at[it, c, k], prev_a[c]),
                )
        ahead(0)
        ahead(1)
        between(0)
        for k in range(4):
            for c in range(2):
                up, down = chunk(k, c, 1), chunk(k, c, 3)
                first[k, c][0].wait_recv()
                part[it, up, c, 0:half, :] = part[it, up, c, 0:half, :] + r1[it, c, k]
                a = send(part.at[it, up, c].at[lo], r2.at[it, c, k].at[lo], next_a[c])
                first[k, c][1].wait_recv()
                part[it, down, c, half:tile, :] = part[it, down, c, half:tile, :] + l1[it, c, k]
                b = send(part.at[it, down, c].at[hi], l2.at[it, c, k].at[hi], prev_a[c])
                second[k, c] = (a, b)
            if k < 2:
                ahead(k + 2)
            between(1 + k)
        for k in range(4):
            for c in range(2):
                for copy in early[k, c] + second[k, c]:
                    copy.wait_recv()
                own = chunk(k, c, 0)
                mid[it, c, k] = part[it, own, c] + r2[it, c, k] + l2[it, c, k]
                if k < 3:
                    third[c].append(
                        send(mid.at[it, c, k], near.at[it, c, k], peers_b[OFF[k]][c])
                    )
            between(5 + k)
        return third

    def finish_sum(it, c, third):
        for copy in third[c]:
            copy.wait_recv()
        return (mid[it, c, 3] + near[it, c, 0]) + (near[it, c, 1] + near[it, c, 2])

    def gather_start(it, c):
        own = panel.at[it, me_c, c]
        deep = [send(own, own, peers_b[OFF[k]][c]) for k in range(3)]
        wide = [send(own, own, peers_a[OFF[k]][c]) for k in range(3)]
        return deep, wide

    def gather_rest(it, starts):
        wide = []
        for k in (1, 2, 0):
            for c in range(2):
                starts[c][0][k].wait_recv()
                piece = panel.at[it, blk(c, pos_b[c] + SIDE - OFF[k], pos_a[c]), c]
                wide += [send(piece, piece, peers_a[OFF[j]][c]) for j in range(3)]
        for copy in starts[0][1] + starts[1][1] + wide:
            copy.wait_recv()

    def forward(it, r):
        acc = None
        for t in range(slots):
            prod = jnp.dot(
                tiles[t], panel_at(it, cols[t]), preferred_element_type=F32
            )
            prod = prod * hot[r][t]
            acc = prod if acc is None else acc + prod
        return acc

    def panel_at(it, col):
        return panel[it, col // 2, col % 2]

    chain[slots] = jnp.zeros((tile, tile), F32)
    loads[0].wait()
    loads[1].wait()
    adjoint(0)
    loads[5].wait()
    pl.semaphore_wait(barrier, n_row - 1 + 4)

    def row_copy(src, dst, group, i):
        return pltpu.make_async_remote_copy(
            src_ref=src,
            dst_ref=dst,
            send_sem=z_send.at[group],
            recv_sem=z_recv.at[group],
            device_id=(me_c, lax.rem(me_r + i, n_row)),
            device_id_type=MESH,
        )

    def send_in(n, carry):
        i = far_first(n)
        row_copy(zs.at[lax.rem(me_r + i, n_row)], zr.at[me_r], 0, i).start()
        return carry

    def wait_rows(buf, group):
        everything = buf.at[pl.ds(0, n_row - 1)]
        pltpu.make_async_copy(everything, everything, z_recv.at[group]).wait()

    def wait_rows_sent(buf, group):
        everything = buf.at[pl.ds(0, n_row - 1)]
        pltpu.make_async_copy(everything, everything, z_send.at[group]).wait()

    blocks = n_row // 2

    def owned(c):
        span = pl.ds(c * blocks, blocks)
        high = zr[span, 0:st_local, :].reshape(tile, tile)
        low = zr[span, st_local : 2 * st_local, :].reshape(tile, tile)
        rest_bits = BOUND[2] - SPLIT
        bound = (high & ((1 << SPLIT) - 1)) * (1 << rest_bits) + (low >> PRIMAL[2])
        start = low & ((1 << PRIMAL[2]) - 1)
        return (
            unfixed(start, PRIMAL),
            unfixed(high >> SPLIT, COST),
            unfixed(bound, BOUND),
        )

    lax.fori_loop(1, n_row, send_in, 0)
    zr[me_r] = zs[me_r]
    third = scatter_sum(0, lambda stage: None)
    wait_rows(zr, 0)
    starts = {}
    p_change = None
    for c in range(2):
        adj = finish_sum(0, c, third)
        old, cost, bound = owned(c)
        new = jnp.minimum(jnp.maximum(old - step_scale * (cost - adj), 0.0), bound)
        newp[0, c] = new
        panel[0, me_c, c] = (2.0 * new - old).astype(BF16)
        starts[c] = gather_start(0, c)
        moved = jnp.sum((new - old) ** 2, axis=0, keepdims=True)
        p_change = moved if p_change is None else p_change + moved
    gather_rest(0, starts)
    d_change = None
    for r in range(2):
        old = dual_in[r]
        new = jnp.maximum(old + step_scale * (demand_in[r] - forward(0, r)), 0.0)
        dual_out[r] = new
        moved = jnp.sum((new - old) ** 2, axis=0, keepdims=True)
        d_change = moved if d_change is None else d_change + moved
    lane = lax.broadcasted_iota(jnp.int32, (1, tile), 1)
    p_change = p_change + pltpu.roll(p_change, tile // 2, 1)
    d_change = d_change + pltpu.roll(d_change, tile // 2, 1)
    ar_s[0] = jnp.where(lane < tile // 2, p_change, d_change)

    def send_change(n, carry):
        i = far_first(n)
        row_copy(ar_s.at[0], ar1.at[me_r], 1, i).start()
        return carry

    lax.fori_loop(1, n_row, send_change, 0)
    ar1[me_r] = ar_s[0]

    adjoint(1)
    counter[0] = MSGS

    def cons_copy(i):
        return pltpu.make_async_remote_copy(
            src_ref=ar_s.at[1],
            dst_ref=ar2.at[me_c],
            send_sem=z_send.at[3],
            recv_sem=z_recv.at[3],
            device_id=(lax.rem(me_c + i, n_cons), me_r),
            device_id_type=MESH,
        )

    def send_cons(i, carry):
        cons_copy(i).start()
        return carry

    def between_second(stage):
        if stage == 6:
            wait_rows(ar1, 1)
            total = jnp.sum(ar1[...], axis=0)
            ar_s[1] = total
            ar2[me_c] = total
            lax.fori_loop(1, n_cons, send_cons, 0)

    third = scatter_sum(1, between_second)
    others = ar2.at[pl.ds(0, n_cons - 1)]
    pltpu.make_async_copy(others, others, z_recv.at[3]).wait()
    total = jnp.sum(ar2[...], axis=0)
    p_total = jnp.sum(jnp.where(lane < tile // 2, total, 0.0), axis=1, keepdims=True)
    d_total = jnp.sum(jnp.where(lane < tile // 2, 0.0, total), axis=1, keepdims=True)
    ratio = jnp.sqrt(jnp.sqrt((d_total + 1e-06) / (p_total + 1e-06)))
    p_step = step_scale / ratio
    d_step = step_scale * ratio
    for c in range(2):
        adj = finish_sum(1, c, third)
        old = newp[0, c]
        _, cost, bound = owned(c)
        new = jnp.minimum(jnp.maximum(old - p_step * (cost - adj), 0.0), bound)
        newp[1, c] = new
        panel[1, me_c, c] = (2.0 * new - old).astype(BF16)
        starts[c] = gather_start(1, c)

    def result_block(j):
        return newp.at[1, j // blocks, pl.ds((j % blocks) * st_local, st_local)]

    def send_out(n, carry):
        i = far_first(n)
        row_copy(
            result_block(lax.rem(me_r + i, n_row)),
            outb.at[pl.ds(pl.multiple_of(me_r * st_local, st_local), st_local)],
            2,
            i,
        ).start()
        return carry

    lax.fori_loop(1, n_row, send_out, 0)
    outb[pl.ds(pl.multiple_of(me_r * st_local, st_local), st_local), :] = newp[
        1, me_r // blocks, pl.ds(pl.multiple_of((me_r % blocks) * st_local, st_local), st_local), :
    ]
    gather_rest(1, starts)
    for r in range(2):
        dual_out[r] = jnp.maximum(
            dual_out[r] + d_step * (demand_in[r] - forward(1, r)), 0.0
        )
    everything = outb.at[pl.ds(0, (n_row - 1) * st_local)]
    pltpu.make_async_copy(everything, everything, z_recv.at[2]).wait()
    for s in range(st_local):
        primal_out[s * n_row : (s + 1) * n_row, :] = outb[pl.ds(s, n_row, stride=st_local), :]
    for copy in pending:
        copy.wait_send()
    wait_rows_sent(zs, 0)
    wait_rows_sent(ar1, 1)
    pltpu.make_async_copy(others, others, z_send.at[3]).wait()
    pltpu.make_async_copy(everything, everything, z_send.at[2]).wait()


def pin(array):
    return pltpu.with_memory_space_constraint(array, pltpu.MemorySpace.HBM)


def body(
    start_primal,
    start_dual,
    unit_cost,
    upper_bound,
    demand,
    tile_values,
    tile_rows,
    tile_cols,
    tile_count,
):
    st_local, sku_local, scenes = start_primal.shape
    n_row = lax.axis_size("row")
    n_cons = lax.axis_size("cons")
    stores = st_local * n_row
    tile = tile_values.shape[1]
    slots = tile_values.shape[0]
    flat = (st_local * sku_local, scenes)
    smem = pl.BlockSpec(memory_space=pltpu.SMEM)
    vmem = pl.BlockSpec(memory_space=pltpu.VMEM)
    primal, dual = pl.pallas_call(
        functools.partial(kernel, n_row, n_cons, slots),
        out_shape=(
            jax.ShapeDtypeStruct(flat, F32),
            jax.ShapeDtypeStruct(start_dual.shape, F32),
        ),
        in_specs=[smem, smem, smem] + [pl.BlockSpec(memory_space=pltpu.MemorySpace.HBM)] * 6,
        out_specs=(vmem, vmem),
        scratch_shapes=[
            pltpu.VMEM((n_row, 2 * st_local, scenes), jnp.int32),
            pltpu.VMEM((n_row, 2 * st_local, scenes), jnp.int32),
            pltpu.VMEM((slots + 1, tile, scenes), F32),
            pltpu.VMEM((2, n_cons, 2, tile, scenes), F32),
            pltpu.VMEM((2, 2, 4, tile // 2, scenes), F32),
            pltpu.VMEM((2, 2, 4, tile // 2, scenes), F32),
            pltpu.VMEM((2, 2, 4, tile, scenes), F32),
            pltpu.VMEM((2, 2, 4, tile, scenes), F32),
            pltpu.VMEM((2, 2, 4, tile, scenes), F32),
            pltpu.VMEM((2, 2, 3, tile, scenes), F32),
            pltpu.VMEM((2, n_cons, 2, tile, scenes), BF16),
            pltpu.VMEM((2, 2, tile, scenes), F32),
            pltpu.VMEM((stores, scenes), F32),
            pltpu.VMEM((2, 2, tile, scenes), BF16),
            pltpu.VMEM((2, 1, scenes), F32),
            pltpu.VMEM((n_row, 1, scenes), F32),
            pltpu.VMEM((n_cons, 1, scenes), F32),
            pltpu.SemaphoreType.DMA((2 * MSGS,)),
            pltpu.SemaphoreType.DMA((2 * MSGS,)),
            pltpu.SemaphoreType.DMA((4,)),
            pltpu.SemaphoreType.DMA((4,)),
            pltpu.VMEM(flat, F32),
            pltpu.VMEM(flat, F32),
            pltpu.VMEM(flat, F32),
            pltpu.VMEM(start_dual.shape, F32),
            pltpu.VMEM(demand.shape, F32),
            pltpu.VMEM(tile_values.shape, BF16),
            pltpu.SemaphoreType.DMA((6,)),
        ],
        compiler_params=pltpu.CompilerParams(
            collective_id=0, has_side_effects=True, vmem_limit_bytes=50_000_000
        ),
    )(
        tile_rows,
        tile_cols,
        tile_count,
        pin(start_primal.reshape(flat)),
        pin(unit_cost.reshape(flat)),
        pin(upper_bound.reshape(flat)),
        pin(start_dual),
        pin(demand),
        pin(tile_values),
    )
    return (primal.reshape(start_primal.shape), dual)


def solution(mesh):
    placed = (
        P("row", "cons", None),
        P(("cons", "row"), None, None),
        P("row", "cons", None),
        P("row", "cons", None),
        P(("cons", "row"), None, None),
        P(("cons", "row"), None, None),
        P(("cons", "row")),
        P(("cons", "row")),
        P(("cons", "row")),
    )
    return jax.shard_map(
        body,
        mesh=mesh,
        in_specs=placed,
        out_specs=(P("row", "cons", None), P(("cons", "row"), None, None)),
        check_vma=False,
    )
```

```python
import functools

import jax
import jax.numpy as jnp
from jax import lax
from jax.experimental import pallas as pl
from jax.experimental.pallas import tpu as pltpu
from jax.sharding import PartitionSpec as P

ITERS = 2
step_scale = 0.9
SIDE = 4
MESH = pl.DeviceIdType.MESH
F32 = jnp.float32
BF16 = jnp.bfloat16
MSGS = 84


PRIMAL = (0.0, 1.0, 20)
COST = (-6.0, 6.0, 22)
BOUND = (0.5, 2.0, 20)
SPLIT = 9


def fixed(value, form):
    low, high, bits = form
    top = float((1 << bits) - 1)
    code = (value - low) * (top / (high - low)) + 0.5
    return jnp.clip(code, 0.0, top).astype(jnp.int32)


def unfixed(code, form):
    low, high, bits = form
    return code.astype(F32) * ((high - low) / float((1 << bits) - 1)) + low


def kernel(
    n_row,
    n_cons,
    slots,
    rows_ref,
    cols_ref,
    count_ref,
    primal_hbm,
    cost_hbm,
    bound_hbm,
    dual_hbm,
    demand_hbm,
    tiles_hbm,
    primal_out,
    dual_out,
    zs,
    zr,
    chain,
    part,
    r1,
    l1,
    r2,
    l2,
    mid,
    near,
    panel,
    newp,
    outb,
    dlow,
    ar_s,
    ar1,
    ar2,
    send_sem,
    recv_sem,
    z_send,
    z_recv,
    primal_in,
    cost_in,
    bound_in,
    dual_in,
    demand_in,
    tiles,
    in_sem,
):
    loads = [
        pltpu.make_async_copy(src, dst, in_sem.at[i])
        for i, (src, dst) in enumerate(
            (
                (dual_hbm, dual_in),
                (tiles_hbm, tiles),
                (primal_hbm, primal_in),
                (cost_hbm, cost_in),
                (bound_hbm, bound_in),
                (demand_hbm, demand_in),
            )
        )
    ]
    for load in loads:
        load.start()
    st_local = primal_in.shape[0] // n_row
    tile = tiles.shape[1]
    half = tile // 2
    me_c = lax.axis_index("cons")
    me_r = lax.axis_index("row")
    y = me_c // SIDE
    x = me_c % SIDE

    def at_xy(yy, xx):
        return lax.rem(yy, SIDE) * SIDE + lax.rem(xx, SIDE)

    x_next, x_prev = at_xy(y, x + 1), at_xy(y, x + 3)
    y_next, y_prev = at_xy(y + 1, x), at_xy(y + 3, x)
    pos_a, pos_b = (x, y), (y, x)
    next_a, prev_a = (x_next, y_next), (x_prev, y_prev)

    def blk(color, b, a):
        return at_xy(b, a) if color == 0 else at_xy(a, b)

    def far_first(i):
        step = i // 2
        return n_row // 2 + step - 2 * step * (i % 2)

    barrier = pltpu.get_barrier_semaphore()

    def greet(n, carry):
        peer = lax.rem(me_r + far_first(n), n_row)
        pl.semaphore_signal(barrier, inc=1, device_id=(me_c, peer), device_id_type=MESH)
        return carry

    lax.fori_loop(1, n_row, greet, 0)
    for peer in (x_next, x_prev, y_next, y_prev):
        pl.semaphore_signal(barrier, inc=1, device_id=(peer, me_r), device_id_type=MESH)

    pending = []
    counter = [0]

    def send(src, dst, target):
        i = counter[0]
        counter[0] += 1
        copy = pltpu.make_async_remote_copy(
            src_ref=src,
            dst_ref=dst,
            send_sem=send_sem.at[i],
            recv_sem=recv_sem.at[i],
            device_id=(target, me_r),
            device_id_type=MESH,
        )
        copy.start()
        pending.append(copy)
        return copy

    count = count_ref[0]
    rows = [rows_ref[t] for t in range(slots)]
    cols = [cols_ref[t] for t in range(slots)]
    live = [jnp.where(t < count, cols[t], -1) for t in range(slots)]
    before = []
    for t in range(slots):
        found = jnp.int32(slots)
        for u in range(t):
            found = jnp.where(cols[u] == cols[t], u, found)
        before.append(found)
    last_tile = []
    for b in range(2 * n_cons):
        found = jnp.int32(slots)
        for t in range(slots):
            found = jnp.where(live[t] == b, t, found)
        last_tile.append(found)
    hot = [
        [jnp.where((rows[t] == r) & (t < count), 1.0, 0.0).astype(F32) for t in range(slots)]
        for r in range(2)
    ]

    for load in loads[2:5]:
        load.wait()
    for j in range(n_row):
        stores = pl.ds(j, st_local, stride=n_row)
        start = fixed(primal_in[stores, :], PRIMAL)
        cost = fixed(cost_in[stores, :], COST)
        bound = fixed(bound_in[stores, :], BOUND)
        zs[j, 0:st_local, :] = cost * (1 << SPLIT) + (bound >> (BOUND[2] - SPLIT))
        rest = bound & ((1 << (BOUND[2] - SPLIT)) - 1)
        zs[j, st_local : 2 * st_local, :] = rest * (1 << PRIMAL[2]) + start

    def adjoint(it):
        for r in range(2):
            src = dual_in if it == 0 else dual_out
            dlow[it, r] = src[r].astype(BF16)
        for t in range(slots):
            prod = lax.dot_general(
                tiles[t], dlow[it, rows[t]], (((0,), (0,)), ((), ())), preferred_element_type=F32
            )
            chain[t] = prod + chain[before[t]]
        for b in range(2 * n_cons):
            part[it, b // 2, b % 2] = chain[last_tile[b]]

    OFF = (2, 1, 3, 0)
    peers_a = [[at_xy(y, x + o), at_xy(y + o, x)] for o in range(SIDE)]
    peers_b = [[at_xy(y + o, x), at_xy(y, x + o)] for o in range(SIDE)]

    def scatter_sum(it, between):
        lo, hi = pl.ds(0, half), pl.ds(half, half)
        first, early, second = {}, {}, {}
        third = {0: [], 1: []}

        def chunk(k, c, step):
            return blk(c, pos_b[c] + OFF[k], pos_a[c] + step)

        def ahead(k):
            for c in range(2):
                up = part.at[it, chunk(k, c, 1), c]
                down = part.at[it, chunk(k, c, 3), c]
                early[k, c] = (
                    send(up.at[hi], r2.at[it, c, k].at[hi], next_a[c]),
                    send(down.at[lo], l2.at[it, c, k].at[lo], prev_a[c]),
                )

        def across(k):
            for c in range(2):
                opp = part.at[it, chunk(k, c, 2), c]
                first[k, c] = (
                    send(opp.at[lo], r1.at[it, c, k], next_a[c]),
                    send(opp.at[hi], l1.at[it, c, k], prev_a[c]),
                )

        def relay(k):
            for c in range(2):
                up, down = chunk(k, c, 1), chunk(k, c, 3)
                first[k, c][0].wait_recv()
                part[it, up, c, 0:half, :] = part[it, up, c, 0:half, :] + r1[it, c, k]
                a = send(part.at[it, up, c].at[lo], r2.at[it, c, k].at[lo], next_a[c])
                first[k, c][1].wait_recv()
                part[it, down, c, half:tile, :] = part[it, down, c, half:tile, :] + l1[it, c, k]
                b = send(part.at[it, down, c].at[hi], l2.at[it, c, k].at[hi], prev_a[c])
                second[k, c] = (a, b)

        def combine(k):
            for c in range(2):
                for copy in early[k, c] + second[k, c]:
                    copy.wait_recv()
                own = chunk(k, c, 0)
                mid[it, c, k] = part[it, own, c] + r2[it, c, k] + l2[it, c, k]
                if k < 3:
                    third[c].append(
                        send(mid.at[it, c, k], near.at[it, c, k], peers_b[OFF[k]][c])
                    )

        across(0)
        across(1)
        across(2)
        ahead(0)
        ahead(1)
        relay(0)
        ahead(2)
        relay(1)
        relay(2)
        across(3)
        ahead(3)
        combine(0)
        combine(1)
        between()
        combine(2)
        relay(3)
        combine(3)
        return third

    def finish_sum(it, c, third):
        for copy in third[c]:
            copy.wait_recv()
        return (mid[it, c, 3] + near[it, c, 0]) + (near[it, c, 1] + near[it, c, 2])

    def gather_start(it, c):
        own = panel.at[it, me_c, c]
        deep = [send(own, own, peers_b[OFF[k]][c]) for k in range(3)]
        wide = [send(own, own, peers_a[OFF[k]][c]) for k in range(3)]
        return deep, wide

    def gather_rest(it, starts):
        wide = []
        for k in (1, 2, 0):
            for c in range(2):
                starts[c][0][k].wait_recv()
                piece = panel.at[it, blk(c, pos_b[c] + SIDE - OFF[k], pos_a[c]), c]
                wide += [send(piece, piece, peers_a[OFF[j]][c]) for j in range(3)]
        for copy in starts[0][1] + starts[1][1] + wide:
            copy.wait_recv()

    def forward(it, r):
        acc = None
        for t in range(slots):
            prod = jnp.dot(
                tiles[t], panel_at(it, cols[t]), preferred_element_type=F32
            )
            prod = prod * hot[r][t]
            acc = prod if acc is None else acc + prod
        return acc

    def panel_at(it, col):
        return panel[it, col // 2, col % 2]

    chain[slots] = jnp.zeros((tile, tile), F32)
    loads[0].wait()
    loads[1].wait()
    adjoint(0)
    loads[5].wait()
    pl.semaphore_wait(barrier, n_row - 1 + 4)

    def row_copy(src, dst, group, i):
        return pltpu.make_async_remote_copy(
            src_ref=src,
            dst_ref=dst,
            send_sem=z_send.at[group],
            recv_sem=z_recv.at[group],
            device_id=(me_c, lax.rem(me_r + i, n_row)),
            device_id_type=MESH,
        )

    def send_in(n, carry):
        i = far_first(n)
        row_copy(zs.at[lax.rem(me_r + i, n_row)], zr.at[me_r], 0, i).start()
        return carry

    def wait_rows(buf, group):
        everything = buf.at[pl.ds(0, n_row - 1)]
        pltpu.make_async_copy(everything, everything, z_recv.at[group]).wait()

    def wait_rows_sent(buf, group):
        everything = buf.at[pl.ds(0, n_row - 1)]
        pltpu.make_async_copy(everything, everything, z_send.at[group]).wait()

    blocks = n_row // 2

    def owned(c):
        span = pl.ds(c * blocks, blocks)
        high = zr[span, 0:st_local, :].reshape(tile, tile)
        low = zr[span, st_local : 2 * st_local, :].reshape(tile, tile)
        rest_bits = BOUND[2] - SPLIT
        bound = (high & ((1 << SPLIT) - 1)) * (1 << rest_bits) + (low >> PRIMAL[2])
        start = low & ((1 << PRIMAL[2]) - 1)
        return (
            unfixed(start, PRIMAL),
            unfixed(high >> SPLIT, COST),
            unfixed(bound, BOUND),
        )

    lax.fori_loop(1, n_row, send_in, 0)
    zr[me_r] = zs[me_r]
    third = scatter_sum(0, lambda: None)
    wait_rows(zr, 0)
    starts = {}
    p_change = None
    for c in range(2):
        adj = finish_sum(0, c, third)
        old, cost, bound = owned(c)
        new = jnp.minimum(jnp.maximum(old - step_scale * (cost - adj), 0.0), bound)
        newp[0, c] = new
        panel[0, me_c, c] = (2.0 * new - old).astype(BF16)
        starts[c] = gather_start(0, c)
        moved = jnp.sum((new - old) ** 2, axis=0, keepdims=True)
        p_change = moved if p_change is None else p_change + moved
    gather_rest(0, starts)
    d_change = None
    for r in range(2):
        old = dual_in[r]
        new = jnp.maximum(old + step_scale * (demand_in[r] - forward(0, r)), 0.0)
        dual_out[r] = new
        moved = jnp.sum((new - old) ** 2, axis=0, keepdims=True)
        d_change = moved if d_change is None else d_change + moved
    lane = lax.broadcasted_iota(jnp.int32, (1, tile), 1)
    p_change = p_change + pltpu.roll(p_change, tile // 2, 1)
    d_change = d_change + pltpu.roll(d_change, tile // 2, 1)
    ar_s[0] = jnp.where(lane < tile // 2, p_change, d_change)

    def send_change(n, carry):
        i = far_first(n)
        row_copy(ar_s.at[0], ar1.at[me_r], 1, i).start()
        return carry

    lax.fori_loop(1, n_row, send_change, 0)
    ar1[me_r] = ar_s[0]

    adjoint(1)
    counter[0] = MSGS

    def cons_copy(i):
        return pltpu.make_async_remote_copy(
            src_ref=ar_s.at[1],
            dst_ref=ar2.at[me_c],
            send_sem=z_send.at[3],
            recv_sem=z_recv.at[3],
            device_id=(lax.rem(me_c + i, n_cons), me_r),
            device_id_type=MESH,
        )

    def send_cons(i, carry):
        cons_copy(i).start()
        return carry

    def between_second():
        wait_rows(ar1, 1)
        total = jnp.sum(ar1[...], axis=0)
        ar_s[1] = total
        ar2[me_c] = total
        lax.fori_loop(1, n_cons, send_cons, 0)

    third = scatter_sum(1, between_second)
    others = ar2.at[pl.ds(0, n_cons - 1)]
    pltpu.make_async_copy(others, others, z_recv.at[3]).wait()
    total = jnp.sum(ar2[...], axis=0)
    p_total = jnp.sum(jnp.where(lane < tile // 2, total, 0.0), axis=1, keepdims=True)
    d_total = jnp.sum(jnp.where(lane < tile // 2, 0.0, total), axis=1, keepdims=True)
    ratio = jnp.sqrt(jnp.sqrt((d_total + 1e-06) / (p_total + 1e-06)))
    p_step = step_scale / ratio
    d_step = step_scale * ratio
    for c in range(2):
        adj = finish_sum(1, c, third)
        old = newp[0, c]
        _, cost, bound = owned(c)
        new = jnp.minimum(jnp.maximum(old - p_step * (cost - adj), 0.0), bound)
        newp[1, c] = new
        panel[1, me_c, c] = (2.0 * new - old).astype(BF16)
        starts[c] = gather_start(1, c)

    def result_block(j):
        return newp.at[1, j // blocks, pl.ds((j % blocks) * st_local, st_local)]

    def send_out(n, carry):
        i = far_first(n)
        row_copy(
            result_block(lax.rem(me_r + i, n_row)),
            outb.at[pl.ds(pl.multiple_of(me_r * st_local, st_local), st_local)],
            2,
            i,
        ).start()
        return carry

    lax.fori_loop(1, n_row, send_out, 0)
    outb[pl.ds(pl.multiple_of(me_r * st_local, st_local), st_local), :] = newp[
        1, me_r // blocks, pl.ds(pl.multiple_of((me_r % blocks) * st_local, st_local), st_local), :
    ]
    gather_rest(1, starts)
    for r in range(2):
        dual_out[r] = jnp.maximum(
            dual_out[r] + d_step * (demand_in[r] - forward(1, r)), 0.0
        )
    everything = outb.at[pl.ds(0, (n_row - 1) * st_local)]
    pltpu.make_async_copy(everything, everything, z_recv.at[2]).wait()
    for s in range(st_local):
        primal_out[s * n_row : (s + 1) * n_row, :] = outb[pl.ds(s, n_row, stride=st_local), :]
    for copy in pending:
        copy.wait_send()
    wait_rows_sent(zs, 0)
    wait_rows_sent(ar1, 1)
    pltpu.make_async_copy(others, others, z_send.at[3]).wait()
    pltpu.make_async_copy(everything, everything, z_send.at[2]).wait()


def pin(array):
    return pltpu.with_memory_space_constraint(array, pltpu.MemorySpace.HBM)


def body(
    start_primal,
    start_dual,
    unit_cost,
    upper_bound,
    demand,
    tile_values,
    tile_rows,
    tile_cols,
    tile_count,
):
    st_local, sku_local, scenes = start_primal.shape
    n_row = lax.axis_size("row")
    n_cons = lax.axis_size("cons")
    stores = st_local * n_row
    tile = tile_values.shape[1]
    slots = tile_values.shape[0]
    flat = (st_local * sku_local, scenes)
    smem = pl.BlockSpec(memory_space=pltpu.SMEM)
    vmem = pl.BlockSpec(memory_space=pltpu.VMEM)
    primal, dual = pl.pallas_call(
        functools.partial(kernel, n_row, n_cons, slots),
        out_shape=(
            jax.ShapeDtypeStruct(flat, F32),
            jax.ShapeDtypeStruct(start_dual.shape, F32),
        ),
        in_specs=[smem, smem, smem] + [pl.BlockSpec(memory_space=pltpu.MemorySpace.HBM)] * 6,
        out_specs=(vmem, vmem),
        scratch_shapes=[
            pltpu.VMEM((n_row, 2 * st_local, scenes), jnp.int32),
            pltpu.VMEM((n_row, 2 * st_local, scenes), jnp.int32),
            pltpu.VMEM((slots + 1, tile, scenes), F32),
            pltpu.VMEM((2, n_cons, 2, tile, scenes), F32),
            pltpu.VMEM((2, 2, 4, tile // 2, scenes), F32),
            pltpu.VMEM((2, 2, 4, tile // 2, scenes), F32),
            pltpu.VMEM((2, 2, 4, tile, scenes), F32),
            pltpu.VMEM((2, 2, 4, tile, scenes), F32),
            pltpu.VMEM((2, 2, 4, tile, scenes), F32),
            pltpu.VMEM((2, 2, 3, tile, scenes), F32),
            pltpu.VMEM((2, n_cons, 2, tile, scenes), BF16),
            pltpu.VMEM((2, 2, tile, scenes), F32),
            pltpu.VMEM((stores, scenes), F32),
            pltpu.VMEM((2, 2, tile, scenes), BF16),
            pltpu.VMEM((2, 1, scenes), F32),
            pltpu.VMEM((n_row, 1, scenes), F32),
            pltpu.VMEM((n_cons, 1, scenes), F32),
            pltpu.SemaphoreType.DMA((2 * MSGS,)),
            pltpu.SemaphoreType.DMA((2 * MSGS,)),
            pltpu.SemaphoreType.DMA((4,)),
            pltpu.SemaphoreType.DMA((4,)),
            pltpu.VMEM(flat, F32),
            pltpu.VMEM(flat, F32),
            pltpu.VMEM(flat, F32),
            pltpu.VMEM(start_dual.shape, F32),
            pltpu.VMEM(demand.shape, F32),
            pltpu.VMEM(tile_values.shape, BF16),
            pltpu.SemaphoreType.DMA((6,)),
        ],
        compiler_params=pltpu.CompilerParams(
            collective_id=0, has_side_effects=True, vmem_limit_bytes=50_000_000
        ),
    )(
        pin(tile_rows),
        pin(tile_cols),
        tile_count,
        pin(start_primal.reshape(flat)),
        pin(unit_cost.reshape(flat)),
        pin(upper_bound.reshape(flat)),
        pin(start_dual),
        pin(demand),
        pin(tile_values),
    )
    return (primal.reshape(start_primal.shape), dual)


def solution(mesh):
    placed = (
        P("row", "cons", None),
        P(("cons", "row"), None, None),
        P("row", "cons", None),
        P("row", "cons", None),
        P(("cons", "row"), None, None),
        P(("cons", "row"), None, None),
        P(("cons", "row")),
        P(("cons", "row")),
        P(("cons", "row")),
    )
    return jax.shard_map(
        body,
        mesh=mesh,
        in_specs=placed,
        out_specs=(P("row", "cons", None), P(("cons", "row"), None, None)),
        check_vma=False,
    )
```

```python
import functools

import jax
import jax.numpy as jnp
from jax import lax
from jax.experimental import pallas as pl
from jax.experimental.pallas import tpu as pltpu
from jax.sharding import PartitionSpec as P

ITERS = 2
step_scale = 0.9
SIDE = 4
MESH = pl.DeviceIdType.MESH
F32 = jnp.float32
BF16 = jnp.bfloat16
MSGS = 86


PRIMAL = (0.0, 1.0, 20)
COST = (-6.0, 6.0, 22)
BOUND = (0.5, 2.0, 20)
SPLIT = 9


def fixed(value, form):
    low, high, bits = form
    top = float((1 << bits) - 1)
    code = (value - low) * (top / (high - low)) + 0.5
    return jnp.clip(code, 0.0, top).astype(jnp.int32)


def unfixed(code, form):
    low, high, bits = form
    return code.astype(F32) * ((high - low) / float((1 << bits) - 1)) + low


def kernel(
    n_row,
    n_cons,
    slots,
    rows_ref,
    cols_ref,
    count_ref,
    primal_hbm,
    cost_hbm,
    bound_hbm,
    dual_hbm,
    demand_hbm,
    tiles_hbm,
    primal_out,
    dual_out,
    zs,
    zr,
    chain,
    part,
    r1,
    l1,
    r2,
    l2,
    mid,
    near,
    panel,
    newp,
    outb,
    dlow,
    ar_s,
    ar1,
    ar2,
    send_sem,
    recv_sem,
    z_send,
    z_recv,
    primal_in,
    cost_in,
    bound_in,
    dual_in,
    demand_in,
    tiles,
    in_sem,
):
    loads = [
        pltpu.make_async_copy(src, dst, in_sem.at[i])
        for i, (src, dst) in enumerate(
            (
                (dual_hbm, dual_in),
                (tiles_hbm, tiles),
                (primal_hbm, primal_in),
                (cost_hbm, cost_in),
                (bound_hbm, bound_in),
                (demand_hbm, demand_in),
            )
        )
    ]
    for load in loads:
        load.start()
    st_local = primal_in.shape[0] // n_row
    tile = tiles.shape[1]
    half = tile // 2
    me_c = lax.axis_index("cons")
    me_r = lax.axis_index("row")
    y = me_c // SIDE
    x = me_c % SIDE

    def at_xy(yy, xx):
        return lax.rem(yy, SIDE) * SIDE + lax.rem(xx, SIDE)

    x_next, x_prev = at_xy(y, x + 1), at_xy(y, x + 3)
    y_next, y_prev = at_xy(y + 1, x), at_xy(y + 3, x)
    pos_a, pos_b = (x, y), (y, x)
    next_a, prev_a = (x_next, y_next), (x_prev, y_prev)

    def blk(color, b, a):
        return at_xy(b, a) if color == 0 else at_xy(a, b)

    def far_first(i):
        step = i // 2
        return n_row // 2 + step - 2 * step * (i % 2)

    barrier = pltpu.get_barrier_semaphore()

    def greet(n, carry):
        peer = lax.rem(me_r + far_first(n), n_row)
        pl.semaphore_signal(barrier, inc=1, device_id=(me_c, peer), device_id_type=MESH)
        return carry

    lax.fori_loop(1, n_row, greet, 0)
    for peer in (x_next, x_prev, y_next, y_prev):
        pl.semaphore_signal(barrier, inc=1, device_id=(peer, me_r), device_id_type=MESH)

    pending = []
    counter = [0]

    def send(src, dst, target):
        i = counter[0]
        counter[0] += 1
        copy = pltpu.make_async_remote_copy(
            src_ref=src,
            dst_ref=dst,
            send_sem=send_sem.at[i],
            recv_sem=recv_sem.at[i],
            device_id=(target, me_r),
            device_id_type=MESH,
        )
        copy.start()
        pending.append(copy)
        return copy

    count = count_ref[0]
    rows = [rows_ref[t] for t in range(slots)]
    cols = [cols_ref[t] for t in range(slots)]
    live = [jnp.where(t < count, cols[t], -1) for t in range(slots)]
    before = []
    for t in range(slots):
        found = jnp.int32(slots)
        for u in range(t):
            found = jnp.where(cols[u] == cols[t], u, found)
        before.append(found)
    last_tile = []
    for b in range(2 * n_cons):
        found = jnp.int32(slots)
        for t in range(slots):
            found = jnp.where(live[t] == b, t, found)
        last_tile.append(found)
    hot = [
        [jnp.where((rows[t] == r) & (t < count), 1.0, 0.0).astype(F32) for t in range(slots)]
        for r in range(2)
    ]

    for load in loads[2:5]:
        load.wait()
    for j in range(n_row):
        stores = pl.ds(j, st_local, stride=n_row)
        start = fixed(primal_in[stores, :], PRIMAL)
        cost = fixed(cost_in[stores, :], COST)
        bound = fixed(bound_in[stores, :], BOUND)
        zs[j, 0:st_local, :] = cost * (1 << SPLIT) + (bound >> (BOUND[2] - SPLIT))
        rest = bound & ((1 << (BOUND[2] - SPLIT)) - 1)
        zs[j, st_local : 2 * st_local, :] = rest * (1 << PRIMAL[2]) + start

    def adjoint(it):
        for r in range(2):
            src = dual_in if it == 0 else dual_out
            dlow[it, r] = src[r].astype(BF16)
        for t in range(slots):
            prod = lax.dot_general(
                tiles[t], dlow[it, rows[t]], (((0,), (0,)), ((), ())), preferred_element_type=F32
            )
            chain[t] = prod + chain[before[t]]
        for b in range(2 * n_cons):
            part[it, b // 2, b % 2] = chain[last_tile[b]]

    OFF = (2, 1, 3, 0)
    peers_a = [[at_xy(y, x + o), at_xy(y + o, x)] for o in range(SIDE)]
    peers_b = [[at_xy(y + o, x), at_xy(y, x + o)] for o in range(SIDE)]

    def scatter_sum(it, begin, between):
        lo, hi = pl.ds(0, half), pl.ds(half, half)
        first, early, second = {}, {}, {}
        third = {0: [], 1: []}

        def chunk(k, c, step):
            return blk(c, pos_b[c] + OFF[k], pos_a[c] + step)

        def ahead(k):
            for c in range(2):
                up = part.at[it, chunk(k, c, 1), c]
                down = part.at[it, chunk(k, c, 3), c]
                early[k, c] = (
                    send(up.at[hi], r2.at[it, c, k].at[hi], next_a[c]),
                    send(down.at[lo], l2.at[it, c, k].at[lo], prev_a[c]),
                )

        def across(k):
            for c in range(2):
                opp = part.at[it, chunk(k, c, 2), c]
                first[k, c] = (
                    send(opp.at[lo], r1.at[it, c, k], next_a[c]),
                    send(opp.at[hi], l1.at[it, c, k], prev_a[c]),
                )

        def relay(k):
            for c in range(2):
                up, down = chunk(k, c, 1), chunk(k, c, 3)
                first[k, c][0].wait_recv()
                part[it, up, c, 0:half, :] = part[it, up, c, 0:half, :] + r1[it, c, k]
                a = send(part.at[it, up, c].at[lo], r2.at[it, c, k].at[lo], next_a[c])
                first[k, c][1].wait_recv()
                part[it, down, c, half:tile, :] = part[it, down, c, half:tile, :] + l1[it, c, k]
                b = send(part.at[it, down, c].at[hi], l2.at[it, c, k].at[hi], prev_a[c])
                second[k, c] = (a, b)

        def combine(k):
            for c in range(2):
                for copy in early[k, c] + second[k, c]:
                    copy.wait_recv()
                own = chunk(k, c, 0)
                mid[it, c, k] = part[it, own, c] + r2[it, c, k] + l2[it, c, k]
                if k < 3:
                    third[c].append(
                        send(mid.at[it, c, k], near.at[it, c, k], peers_b[OFF[k]][c])
                    )

        across(0)
        across(1)
        across(2)
        ahead(0)
        ahead(1)
        begin()
        relay(0)
        ahead(2)
        relay(1)
        relay(2)
        across(3)
        ahead(3)
        combine(0)
        combine(1)
        between()
        combine(2)
        relay(3)
        combine(3)
        return third

    def finish_sum(it, c, third):
        for copy in third[c]:
            copy.wait_recv()
        return (mid[it, c, 3] + near[it, c, 0]) + (near[it, c, 1] + near[it, c, 2])

    def gather_start(it, c):
        own = panel.at[it, me_c, c]
        deep = [send(own, own, peers_b[OFF[k]][c]) for k in range(3)]
        wide = [send(own, own, peers_a[OFF[k]][c]) for k in (1, 2)]
        return deep, wide

    def gather_rest(it, starts):
        wide = []
        for k in (1, 2, 0):
            for c in range(2):
                starts[c][0][k].wait_recv()
                piece = panel.at[it, blk(c, pos_b[c] + SIDE - OFF[k], pos_a[c]), c]
                wide += [send(piece, piece, peers_a[OFF[j]][c]) for j in range(3)]
            if k == 1:
                for c in range(2):
                    from_prev, from_next = starts[c][1]
                    from_prev.wait_recv()
                    piece = panel.at[it, blk(c, pos_b[c], pos_a[c] + 3), c].at[pl.ds(0, half)]
                    wide.append(send(piece, piece, next_a[c]))
                    from_next.wait_recv()
                    piece = panel.at[it, blk(c, pos_b[c], pos_a[c] + 1), c].at[pl.ds(half, half)]
                    wide.append(send(piece, piece, prev_a[c]))
        for copy in wide:
            copy.wait_recv()

    def forward(it):
        sums = [None, None]
        for t in range(slots):
            prod = jnp.dot(tiles[t], panel_at(it, cols[t]), preferred_element_type=F32)
            for r in range(2):
                term = prod * hot[r][t]
                sums[r] = term if t == 0 else sums[r] + term
        return sums

    def panel_at(it, col):
        return panel[it, col // 2, col % 2]

    chain[slots] = jnp.zeros((tile, tile), F32)
    loads[0].wait()
    loads[1].wait()
    adjoint(0)
    loads[5].wait()
    pl.semaphore_wait(barrier, n_row - 1 + 4)

    def row_copy(src, dst, group, i):
        return pltpu.make_async_remote_copy(
            src_ref=src,
            dst_ref=dst,
            send_sem=z_send.at[group],
            recv_sem=z_recv.at[group],
            device_id=(me_c, lax.rem(me_r + i, n_row)),
            device_id_type=MESH,
        )

    def send_in(n, carry):
        i = far_first(n)
        row_copy(zs.at[lax.rem(me_r + i, n_row)], zr.at[me_r], 0, i).start()
        return carry

    def wait_rows(buf, group):
        everything = buf.at[pl.ds(0, n_row - 1)]
        pltpu.make_async_copy(everything, everything, z_recv.at[group]).wait()

    def wait_rows_sent(buf, group):
        everything = buf.at[pl.ds(0, n_row - 1)]
        pltpu.make_async_copy(everything, everything, z_send.at[group]).wait()

    blocks = n_row // 2

    def owned(c):
        span = pl.ds(c * blocks, blocks)
        high = zr[span, 0:st_local, :].reshape(tile, tile)
        low = zr[span, st_local : 2 * st_local, :].reshape(tile, tile)
        rest_bits = BOUND[2] - SPLIT
        bound = (high & ((1 << SPLIT) - 1)) * (1 << rest_bits) + (low >> PRIMAL[2])
        start = low & ((1 << PRIMAL[2]) - 1)
        return (
            unfixed(start, PRIMAL),
            unfixed(high >> SPLIT, COST),
            unfixed(bound, BOUND),
        )

    lax.fori_loop(1, n_row, send_in, 0)
    zr[me_r] = zs[me_r]
    third = scatter_sum(0, lambda: None, lambda: None)
    wait_rows(zr, 0)
    starts = {}
    p_change = None
    for c in range(2):
        adj = finish_sum(0, c, third)
        old, cost, bound = owned(c)
        new = jnp.minimum(jnp.maximum(old - step_scale * (cost - adj), 0.0), bound)
        newp[0, c] = new
        panel[0, me_c, c] = (2.0 * new - old).astype(BF16)
        starts[c] = gather_start(0, c)
        moved = jnp.sum((new - old) ** 2, axis=0, keepdims=True)
        p_change = moved if p_change is None else p_change + moved
    gather_rest(0, starts)
    d_change = None
    product = forward(0)
    for r in range(2):
        old = dual_in[r]
        new = jnp.maximum(old + step_scale * (demand_in[r] - product[r]), 0.0)
        dual_out[r] = new
        moved = jnp.sum((new - old) ** 2, axis=0, keepdims=True)
        d_change = moved if d_change is None else d_change + moved
    lane = lax.broadcasted_iota(jnp.int32, (1, tile), 1)
    p_change = p_change + pltpu.roll(p_change, tile // 2, 1)
    d_change = d_change + pltpu.roll(d_change, tile // 2, 1)
    ar_s[0] = jnp.where(lane < tile // 2, p_change, d_change)

    def send_change(n, carry):
        i = far_first(n)
        row_copy(ar_s.at[0], ar1.at[me_r], 1, i).start()
        return carry

    def begin_second():
        lax.fori_loop(1, n_row, send_change, 0)
        ar1[me_r] = ar_s[0]

    adjoint(1)
    counter[0] = MSGS

    def cons_copy(i):
        return pltpu.make_async_remote_copy(
            src_ref=ar_s.at[1],
            dst_ref=ar2.at[me_c],
            send_sem=z_send.at[3],
            recv_sem=z_recv.at[3],
            device_id=(lax.rem(me_c + i, n_cons), me_r),
            device_id_type=MESH,
        )

    def send_cons(i, carry):
        cons_copy(i).start()
        return carry

    def between_second():
        wait_rows(ar1, 1)
        total = jnp.sum(ar1[...], axis=0)
        ar_s[1] = total
        ar2[me_c] = total
        lax.fori_loop(1, n_cons, send_cons, 0)

    third = scatter_sum(1, begin_second, between_second)
    others = ar2.at[pl.ds(0, n_cons - 1)]
    pltpu.make_async_copy(others, others, z_recv.at[3]).wait()
    total = jnp.sum(ar2[...], axis=0)
    p_total = jnp.sum(jnp.where(lane < tile // 2, total, 0.0), axis=1, keepdims=True)
    d_total = jnp.sum(jnp.where(lane < tile // 2, 0.0, total), axis=1, keepdims=True)
    ratio = jnp.sqrt(jnp.sqrt((d_total + 1e-06) / (p_total + 1e-06)))
    p_step = step_scale / ratio
    d_step = step_scale * ratio
    for c in range(2):
        adj = finish_sum(1, c, third)
        old = newp[0, c]
        _, cost, bound = owned(c)
        new = jnp.minimum(jnp.maximum(old - p_step * (cost - adj), 0.0), bound)
        newp[1, c] = new
        panel[1, me_c, c] = (2.0 * new - old).astype(BF16)
        starts[c] = gather_start(1, c)

    def result_block(j):
        return newp.at[1, j // blocks, pl.ds((j % blocks) * st_local, st_local)]

    def send_out(n, carry):
        i = far_first(n)
        row_copy(
            result_block(lax.rem(me_r + i, n_row)),
            outb.at[pl.ds(pl.multiple_of(me_r * st_local, st_local), st_local)],
            2,
            i,
        ).start()
        return carry

    lax.fori_loop(1, n_row, send_out, 0)
    outb[pl.ds(pl.multiple_of(me_r * st_local, st_local), st_local), :] = newp[
        1, me_r // blocks, pl.ds(pl.multiple_of((me_r % blocks) * st_local, st_local), st_local), :
    ]
    gather_rest(1, starts)
    product = forward(1)
    for r in range(2):
        dual_out[r] = jnp.maximum(
            dual_out[r] + d_step * (demand_in[r] - product[r]), 0.0
        )
    everything = outb.at[pl.ds(0, (n_row - 1) * st_local)]
    pltpu.make_async_copy(everything, everything, z_recv.at[2]).wait()
    for s in range(st_local):
        primal_out[s * n_row : (s + 1) * n_row, :] = outb[pl.ds(s, n_row, stride=st_local), :]
    for copy in pending:
        copy.wait_send()
    wait_rows_sent(zs, 0)
    wait_rows_sent(ar1, 1)
    pltpu.make_async_copy(others, others, z_send.at[3]).wait()
    pltpu.make_async_copy(everything, everything, z_send.at[2]).wait()


def pin(array):
    return pltpu.with_memory_space_constraint(array, pltpu.MemorySpace.HBM)


def body(
    start_primal,
    start_dual,
    unit_cost,
    upper_bound,
    demand,
    tile_values,
    tile_rows,
    tile_cols,
    tile_count,
):
    st_local, sku_local, scenes = start_primal.shape
    n_row = lax.axis_size("row")
    n_cons = lax.axis_size("cons")
    stores = st_local * n_row
    tile = tile_values.shape[1]
    slots = tile_values.shape[0]
    flat = (st_local * sku_local, scenes)
    smem = pl.BlockSpec(memory_space=pltpu.SMEM)
    vmem = pl.BlockSpec(memory_space=pltpu.VMEM)
    primal, dual = pl.pallas_call(
        functools.partial(kernel, n_row, n_cons, slots),
        out_shape=(
            jax.ShapeDtypeStruct(flat, F32),
            jax.ShapeDtypeStruct(start_dual.shape, F32),
        ),
        in_specs=[smem, smem, smem] + [pl.BlockSpec(memory_space=pltpu.MemorySpace.HBM)] * 6,
        out_specs=(vmem, vmem),
        scratch_shapes=[
            pltpu.VMEM((n_row, 2 * st_local, scenes), jnp.int32),
            pltpu.VMEM((n_row, 2 * st_local, scenes), jnp.int32),
            pltpu.VMEM((slots + 1, tile, scenes), F32),
            pltpu.VMEM((2, n_cons, 2, tile, scenes), F32),
            pltpu.VMEM((2, 2, 4, tile // 2, scenes), F32),
            pltpu.VMEM((2, 2, 4, tile // 2, scenes), F32),
            pltpu.VMEM((2, 2, 4, tile, scenes), F32),
            pltpu.VMEM((2, 2, 4, tile, scenes), F32),
            pltpu.VMEM((2, 2, 4, tile, scenes), F32),
            pltpu.VMEM((2, 2, 3, tile, scenes), F32),
            pltpu.VMEM((2, n_cons, 2, tile, scenes), BF16),
            pltpu.VMEM((2, 2, tile, scenes), F32),
            pltpu.VMEM((stores, scenes), F32),
            pltpu.VMEM((2, 2, tile, scenes), BF16),
            pltpu.VMEM((2, 1, scenes), F32),
            pltpu.VMEM((n_row, 1, scenes), F32),
            pltpu.VMEM((n_cons, 1, scenes), F32),
            pltpu.SemaphoreType.DMA((2 * MSGS,)),
            pltpu.SemaphoreType.DMA((2 * MSGS,)),
            pltpu.SemaphoreType.DMA((4,)),
            pltpu.SemaphoreType.DMA((4,)),
            pltpu.VMEM(flat, F32),
            pltpu.VMEM(flat, F32),
            pltpu.VMEM(flat, F32),
            pltpu.VMEM(start_dual.shape, F32),
            pltpu.VMEM(demand.shape, F32),
            pltpu.VMEM(tile_values.shape, BF16),
            pltpu.SemaphoreType.DMA((6,)),
        ],
        compiler_params=pltpu.CompilerParams(
            collective_id=0, has_side_effects=True, vmem_limit_bytes=50_000_000
        ),
    )(
        pin(tile_rows),
        pin(tile_cols),
        tile_count,
        pin(start_primal.reshape(flat)),
        pin(unit_cost.reshape(flat)),
        pin(upper_bound.reshape(flat)),
        pin(start_dual),
        pin(demand),
        pin(tile_values),
    )
    return (primal.reshape(start_primal.shape), dual)


def solution(mesh):
    placed = (
        P("row", "cons", None),
        P(("cons", "row"), None, None),
        P("row", "cons", None),
        P("row", "cons", None),
        P(("cons", "row"), None, None),
        P(("cons", "row"), None, None),
        P(("cons", "row")),
        P(("cons", "row")),
        P(("cons", "row")),
    )
    return jax.shard_map(
        body,
        mesh=mesh,
        in_specs=placed,
        out_specs=(P("row", "cons", None), P(("cons", "row"), None, None)),
        check_vma=False,
    )
```
